32 devices in a mesh: rows: 8 (over z, x), scales: 4 (over y, core).
Axes of the slice: x: 2, y: 2, z: 4, core: 2. Of those that a mesh axis runs over, the one named last changes fastest.
Arguments:
- image_now: float32 [256, 8192], P(('rows', 'scales')), may hold values from 0.1 to 4
- gradient: float32 [256, 8192], P(('rows', 'scales')), may hold values from -140 to 140
- hessian_weight: float32 [256, 8192], P(('rows', 'scales')), may hold values from 0.1 to 10
- psf_tiles: float32 [32, 256], P(('rows', 'scales')), may hold values from -0.5 to 1.7
- facet_of_row: int32 [256], P(('rows', 'scales')), may hold values from 0 to 31, never falling along the last dimension, each value on 1 to 32 neighbouring positions
- tile_slot: int32 [32], replicated, may hold values from 0 to 31, each once
- thresholds: float32 [4], replicated, may hold values from 0.2 to 2
Outputs:
- new_image: float32 [256, 8192], P(('rows', 'scales'))
The draws below stay inside these ranges and needn't reach their ends.
Inputs may be any that keep to these rules, and one draw needn't show every extreme that they name: `facet_of_row`: facet numbers never fall along the rows; every facet covers 1 to 32 rows, and some facet exactly 32. `tile_slot`: each facet's tile stands in a different row of psf_tiles, and every row holds one.
All inputs are finite; a program needn't handle non-finite values.
Results may differ from the reference program's by a relative error of at most 0.0001.
Values sent between devices are 32-bit elements; how exact they have to be, the bound alone decides.
A program may use at most 64 MiB of HBM per device.

```python
import math
import jax
import jax.numpy as jnp
import numpy as np
from jax import lax

COLS = 8192
TILE = 16
SUBITERS = 2
SCALES = 4
HEIGHT = 256
FACETS = 32
FMOST = 32


def draw_gradient(key, part):
    key_noise, key_rows, key_cols = jax.random.split(key, 3)
    position = jnp.arange(HEIGHT, dtype=jnp.float32)[:, None] / HEIGHT
    rising = jnp.exp(math.log(3.0) * position)
    row_scale = jnp.exp(jax.random.uniform(key_rows, (HEIGHT, 1), minval=0.0, maxval=math.log(10.0))) * rising
    col_scale = jnp.exp(jax.random.uniform(key_cols, (1, COLS), minval=0.0, maxval=math.log(10.0)))
    pattern = jnp.clip(jax.random.normal(key_noise, (HEIGHT, COLS)), -6.0, 6.0)
    return (0.03 * pattern * row_scale * col_scale).astype(jnp.float32)


def draw_hessian_weight(key, part):
    key_cells, key_rows = jax.random.split(key, 2)
    cells = jnp.exp(jax.random.uniform(key_cells, (HEIGHT, COLS), minval=math.log(0.1), maxval=0.0))
    row_scale = jnp.exp(jax.random.uniform(key_rows, (HEIGHT, 1), minval=0.0, maxval=math.log(10.0)))
    return (cells * row_scale).astype(jnp.float32)


def draw_psf_tiles(key, part):
    key_side, key_peak = jax.random.split(key, 2)
    centre = (jnp.arange(TILE * TILE) == TILE // 2 * TILE + TILE // 2)[None, :]
    side_lobes = 0.1 * jnp.clip(jax.random.normal(key_side, (FACETS, TILE * TILE)), -4.0, 4.0)
    peak_value = jax.random.uniform(key_peak, (FACETS, 1), minval=0.8, maxval=1.2)
    return jnp.where(centre, peak_value + side_lobes, side_lobes).astype(jnp.float32)


def level_of(key, shape, cuts, least, largest):
    def one(dim, parts):
        heights = jax.random.uniform(jax.random.fold_in(jax.random.fold_in(key, 6), dim), (parts,), jnp.float32, least / len(cuts), largest / len(cuts))
        return jnp.repeat(jnp.exp(heights), shape[dim] // parts).reshape((-1,) + (1,) * (len(shape) - dim - 1))

    gain = one(*cuts[0])
    for cut in cuts[1:]:
        gain = gain * one(*cut)
    return gain


def profile(number_of, total, reach, slope):
    loads = [(1 << 20) // math.isqrt(grade ** slope) + 1 for grade in range(2, number_of + 1)]
    spare, given = total - reach - (number_of - 1), [1] * (number_of - 1)
    while spare > 0:
        movable = [i for i in range(number_of - 1) if given[i] < reach]
        whole, budget = sum([loads[i] for i in movable]), spare
        for i in movable:
            extra = min(reach - given[i], max(1, budget * loads[i] // whole), spare)
            given[i] = given[i] + extra
            spare = spare - extra
    return np.array([reach] + given)


def ragged_sizes(key, count, total, bound, lean):
    if count == 2:
        one = jax.random.randint(key, (), max(1, total - bound), min(bound, total - 1) + 1)
        return jnp.stack([one, total - one])
    sizes = jnp.asarray(profile(count, total, bound, lean), jnp.int32)
    couples = (count - 1) // 2
    source_of, receiver = sizes[1:1 + 2 * couples:2], sizes[2:2 + 2 * couples:2]
    slack = jnp.minimum(source_of - 1, bound - receiver)
    moved = jax.random.randint(jax.random.fold_in(key, 1), (couples,), 0, 1 << 20) % (slack + 1)
    sizes = sizes.at[1:1 + 2 * couples:2].set(source_of - moved).at[2:2 + 2 * couples:2].set(receiver + moved)
    return sizes[jax.random.permutation(jax.random.fold_in(key, 2), count)]


def setup_inputs(seed: int = 0) -> dict:
    streams_of = jax.random.split(jax.random.key(seed), 8)
    return {
        "image_now": jnp.clip(jnp.exp(math.log(4.0) - 3.6888794 * jax.random.uniform(streams_of[0], (HEIGHT, COLS), jnp.float32) ** level_of(streams_of[0], (HEIGHT, COLS), ((0, 32),), -0.2, 0.2)), 0.1, 4.0),
        "gradient": draw_gradient(jax.random.fold_in(streams_of[7], 71), 0),
        "hessian_weight": draw_hessian_weight(jax.random.fold_in(streams_of[7], 71), 0),
        "psf_tiles": draw_psf_tiles(jax.random.fold_in(streams_of[7], 71), 0),
        "facet_of_row": jnp.searchsorted(jnp.cumsum(ragged_sizes(streams_of[4], FACETS, HEIGHT, FMOST, 2)), jnp.arange(HEIGHT), side="right").astype(jnp.int32),
        "tile_slot": jax.random.permutation(streams_of[5], FACETS).astype(jnp.int32),
        "thresholds": jnp.clip(jnp.exp(jax.random.uniform(streams_of[6], (SCALES,), jnp.float32, math.log(0.2), math.log(2.0))), 0.2, 2.0),
    }


SPLINE_EDGE = 0.0625
SPLINE_NEAR = 0.25
SPLINE_MID = 0.375


def along_columns(source, spacing):
    length = source.shape[1]
    padded = jnp.pad(source, ((0, 0), (2 * spacing, 2 * spacing)))
    outer_pair = padded[:, 0:length] + padded[:, 4 * spacing:4 * spacing + length]
    inner_pair = padded[:, spacing:spacing + length] + padded[:, 3 * spacing:3 * spacing + length]
    return SPLINE_EDGE * outer_pair + SPLINE_NEAR * inner_pair + SPLINE_MID * source


def along_rows(source, spacing):
    length = source.shape[0]
    padded = jnp.pad(source, ((2 * spacing, 2 * spacing), (0, 0)))
    outer_pair = padded[0:length] + padded[4 * spacing:4 * spacing + length]
    inner_pair = padded[spacing:spacing + length] + padded[3 * spacing:3 * spacing + length]
    return SPLINE_EDGE * outer_pair + SPLINE_NEAR * inner_pair + SPLINE_MID * source


def forward_blur(source, weights):
    height, columns = source.shape
    half_tile = TILE // 2
    padded = jnp.pad(source, ((half_tile, half_tile), (half_tile, half_tile)))

    def add_tap_row(tap_row, summed):
        shifted = lax.dynamic_slice_in_dim(padded, tap_row, height, 0)
        tap_weights = lax.dynamic_index_in_dim(weights, tap_row, 1, keepdims=False)
        for column in range(TILE):
            summed = summed + tap_weights[:, column:column + 1] * shifted[:, column:column + columns]
        return summed

    return lax.fori_loop(0, TILE, add_tap_row, jnp.zeros((height, columns), jnp.float32))


def adjoint_blur(source, weights):
    height, columns = source.shape
    half_tile = TILE // 2
    padded = jnp.pad(source, ((half_tile, half_tile), (half_tile, half_tile)))
    wide_weights = jnp.pad(weights, ((half_tile, half_tile), (0, 0), (0, 0)))

    def add_tap_row(tap_row, summed):
        offset = 2 * half_tile - tap_row
        shifted = lax.dynamic_slice_in_dim(padded, offset, height, 0)
        weight_rows = lax.dynamic_slice_in_dim(wide_weights, offset, height, 0)
        tap_weights = lax.dynamic_index_in_dim(weight_rows, tap_row, 1, keepdims=False)
        for column in range(TILE):
            offset_col = 2 * half_tile - column
            summed = summed + tap_weights[:, column:column + 1] * shifted[:, offset_col:offset_col + columns]
        return summed

    return lax.fori_loop(0, TILE, add_tap_row, jnp.zeros((height, columns), jnp.float32))


def shrink(trial, step_size, thresholds):
    smooth = trial
    summed = jnp.zeros_like(trial)
    for depth in range(SCALES):
        smoother = along_rows(along_columns(smooth, 2 ** depth), 2 ** depth)
        detail = smooth - smoother
        limit = step_size * thresholds[depth]
        summed = summed + (detail - jnp.clip(detail, -limit, limit))
        smooth = smoother
    return summed + smooth


def reference(image_now, gradient, hessian_weight, psf_tiles, facet_of_row, tile_slot, thresholds):
    slot_rows = jnp.take(tile_slot, facet_of_row).astype(jnp.int32)
    weights = jnp.take(psf_tiles, slot_rows, axis=0).reshape(HEIGHT, TILE, TILE)
    current = image_now
    for sweep in range(SUBITERS):
        change = current - image_now
        pushed = hessian_weight * forward_blur(change, weights)
        descent = gradient + adjoint_blur(pushed, weights)
        blurred = forward_blur(descent, weights)
        step_size = jnp.sum(descent * descent) / jnp.sum(hessian_weight * blurred * blurred)
        current = shrink(current - step_size * descent, step_size, thresholds)
    return current
```

```python
import functools

import jax
import jax.numpy as jnp
import numpy as np
from jax import lax
from jax.experimental import pallas as pl
from jax.experimental.pallas import tpu as pltpu
from jax.sharding import PartitionSpec as P

TILE = 16
HALF = TILE // 2
SUBITERS = 2
LANES = 128
BLOCK = 32
GROUPS = LANES // BLOCK
WIDTH = 8 * BLOCK
AXES = ("rows", "scales")
VMEM = pl.BlockSpec(memory_space=pltpu.VMEM)


def spline_matrices(levels):
    w = np.arange(WIDTH)
    same = (w[:, None] // BLOCK) == (w[None, :] // BLOCK)
    place = w % BLOCK
    nearer = place + np.where(place < BLOCK // 2, BLOCK, -BLOCK)
    planes = []
    for level in range(levels):
        d = 2**level
        for column in (place, nearer):
            o = np.abs(column[:, None] - place[None, :])
            coef = np.where(o == 0, 0.375, np.where(o == d, 0.25, np.where(o == 2 * d, 0.0625, 0.0)))
            planes.append(np.where(same, coef, 0.0))
    return jnp.asarray(np.stack(planes), jnp.bfloat16)


def halves(x):
    high = x.astype(jnp.bfloat16)
    low = (x - high.astype(jnp.float32)).astype(jnp.bfloat16)
    return high, low


def dot(a, b):
    return jnp.dot(a, b, preferred_element_type=jnp.float32)


def block_shift(x, s):
    if s == 0:
        return x
    count = x.shape[0] // GROUPS
    parts = [x[p * count : (p + 1) * count] for p in range(GROUPS)]
    row = lax.broadcasted_iota(jnp.int32, parts[0].shape, 0)
    if s == 1:
        last = jnp.where(row == count - 1, 0.0, pltpu.roll(parts[0], count - 1, 0))
        return jnp.concatenate(parts[1:] + [last], axis=0)
    first = jnp.where(row == 0, 0.0, pltpu.roll(parts[-1], 1, 0))
    return jnp.concatenate([first] + parts[:-1], axis=0)


def beside(x):
    lane = lax.broadcasted_iota(jnp.int32, x.shape, 1) % BLOCK
    return jnp.where(lane < BLOCK // 2, block_shift(x, 1), block_shift(x, -1))


def blur(stripes, high_ref, low_ref):
    total = None
    for t, x in enumerate(stripes):
        for n, y in enumerate((x, beside(x))):
            high, low = halves(y)
            w = high_ref[t * 2 + n]
            part = dot(high, w) + dot(low, w) + dot(high, low_ref[t * 2 + n])
            total = part if total is None else total + part
    return total


def to_blocks(src_ref, dst_ref, tiles):
    count = src_ref.shape[1] // LANES
    for q in range(count):
        tiles[pl.ds(8 * q, 8), :] = src_ref[:, q * LANES : (q + 1) * LANES]
    group = lax.broadcasted_iota(jnp.int32, (count, LANES), 1) // BLOCK
    for half in range(2):
        outs = [None] * GROUPS
        for k in range(4):
            a = tiles[pl.ds(half * 4 + k, count, stride=8), :]
            for p in range(GROUPS):
                shift = BLOCK * ((k - p) % 4)
                moved = pltpu.roll(a, shift, 1) if shift else a
                outs[p] = moved if k == 0 else jnp.where(group == k, moved, outs[p])
        for p in range(GROUPS):
            dst_ref[p * count : (p + 1) * count, half * LANES : (half + 1) * LANES] = outs[p]


def from_blocks(src_ref, dst_ref, tiles):
    count = dst_ref.shape[1] // LANES
    group = lax.broadcasted_iota(jnp.int32, (count, LANES), 1) // BLOCK
    for half in range(2):
        for k in range(4):
            out = None
            for p in range(GROUPS):
                x = src_ref[p * count : (p + 1) * count, half * LANES : (half + 1) * LANES]
                shift = BLOCK * ((p - k) % 4)
                moved = pltpu.roll(x, shift, 1) if shift else x
                out = moved if p == 0 else jnp.where(group == p, moved, out)
            tiles[pl.ds(half * 4 + k, count, stride=8), :] = out
    for q in range(count):
        dst_ref[:, q * LANES : (q + 1) * LANES] = tiles[pl.ds(8 * q, 8), :]


def build_weights(base_ref, lead, high_ref, low_ref, wide):
    lane = lax.broadcasted_iota(jnp.int32, (8, WIDTH), 1) % BLOCK
    for t in range(3):
        base = base_ref[8 * t : 8 * t + 8, :]
        for w in range(BLOCK):
            for n, s in enumerate((0, 1 if w < BLOCK // 2 else -1)):
                moved = pltpu.roll(base, (w - lead + BLOCK * s) % WIDTH, 1)
                x = lane - (w - lead + BLOCK * s)
                kept = jnp.where((x >= 0) & (x < TILE), moved, 0.0)
                for half in range(2):
                    wide[n, half, pl.ds(w, 8, stride=BLOCK), :] = kept[
                        :, half * LANES : (half + 1) * LANES
                    ]
        for n in range(2):
            for half in range(2):
                high, low = halves(wide[n, half])
                high_ref[t * 2 + n, :, half * LANES : (half + 1) * LANES] = high
                low_ref[t * 2 + n, :, half * LANES : (half + 1) * LANES] = low


def moved_rows(vregs, rolls, i, d):
    if d % 4 == 0:
        return vregs[i + d // 4]
    shift = (-BLOCK * d) % LANES

    def rolled(n):
        if (n, shift) not in rolls:
            rolls[(n, shift)] = pltpu.roll(vregs[n], shift, 1)
        return rolls[(n, shift)]

    lane = lax.broadcasted_iota(jnp.int32, vregs[i].shape, 1)
    if d > 0:
        return jnp.where(lane < LANES - BLOCK * d, rolled(i), rolled(i + 1))
    return jnp.where(lane >= -BLOCK * d, rolled(i), rolled(i - 1))


def column_cascade(stripe_refs, alive, levels_ref, step_rows):
    reach = len(stripe_refs) // 2
    levels = levels_ref.shape[0]

    def chunk(n, carry):
        rows = pl.ds(pl.multiple_of(n * step_rows, step_rows), step_rows)
        vregs = {}
        for t, ref in enumerate(stripe_refs):
            for half in range(2):
                vregs[2 * t + half] = ref[rows, half * LANES : (half + 1) * LANES]
        own = 2 * reach
        for level in range(levels):
            d = 2**level
            left = 2 ** (levels + 1) - 2 ** (level + 2)
            margin = -(-left // 4)
            rolls, out = {}, {}
            keys = vregs
            for i in range(own - margin, own + 2 + margin):
                outer = moved_rows(keys, rolls, i, -2 * d) + moved_rows(keys, rolls, i, 2 * d)
                inner = moved_rows(keys, rolls, i, -d) + moved_rows(keys, rolls, i, d)
                value = 0.0625 * outer + 0.25 * inner + 0.375 * keys[i]
                t = i // 2
                out[i] = value if t == reach else value * alive[t]
            vregs = out
            for half in range(2):
                levels_ref[level, rows, half * LANES : (half + 1) * LANES] = out[own + half]
        return carry

    lax.fori_loop(0, stripe_refs[0].shape[0] // step_rows, chunk, 0)


def row_cascade(levels_ref, spline_ref):
    levels = levels_ref.shape[0]
    for level in range(levels):

        def one(k, carry):
            x = levels_ref[k]
            total = None
            for n, y in enumerate((x, beside(x))):
                high, low = halves(y)
                w = spline_ref[level * 2 + n]
                part = dot(high, w) + dot(low, w)
                total = part if total is None else total + part
            levels_ref[k] = total
            return carry

        lax.fori_loop(level, levels, one, 0)


def keep(own, levels_ref, limits):
    levels = levels_ref.shape[0]
    smooth = own
    total = None
    for k in range(levels):
        smoother = levels_ref[k]
        detail = smooth - smoother
        part = detail - jnp.clip(detail, -limits[k], limits[k])
        total = part if total is None else total + part
        smooth = smoother
    return total + smooth


def build_bases(taps, flipped, forward, adjoint):
    lane = lax.broadcasted_iota(jnp.int32, (8, WIDTH), 1)
    sub = lax.broadcasted_iota(jnp.int32, (8, WIDTH), 0)
    group, inside = lane // BLOCK, lane % BLOCK < TILE
    own = flipped[...]
    turned = [pltpu.roll(own, TILE * n, 1) if n else own for n in range(TILE)]
    forward[...] = jnp.zeros_like(forward)
    for a in range(TILE):
        placed = jnp.zeros((8, WIDTH), jnp.float32)
        for r in range(8):
            placed = jnp.where((sub == r) & (group == r) & inside, turned[(2 * r - a) % TILE], placed)
        forward[a : a + 8, :] += placed
    for t in range(3):
        x = taps[t]
        row = sub + 8 * t
        tap = group - row + TILE
        placed = jnp.zeros((8, WIDTH), jnp.float32)
        for n in range(TILE):
            moved = pltpu.roll(x, TILE * n, 1) if n else x
            use = ((group + row) % TILE == n) & inside & (tap >= 0) & (tap < TILE)
            placed = jnp.where(use, moved, placed)
        adjoint[8 * t : 8 * t + 8, :] = placed


def stripe_kernel(
    count, scales, side,
    image, gradient, weight, psf, facet, slot_of, thresholds, spline,
    out,
    xi, xg, xh, current, near, middle, far, psf_all, taps, flipped, base_f, base_a, fh, fl, ah, al,
    levels, sums, tiles, wide,
    psf_send, psf_recv, sum_send, sum_recv, tap_send, tap_recv, near_send, near_recv, far_send, far_recv,
):
    me = lax.axis_index("rows") * scales + lax.axis_index("scales")
    barrier = pltpu.get_barrier_semaphore()

    def device(index):
        return (index // scales, index % scales)

    def peer(k):
        return (me + k) % count

    def exists(o):
        return (me + o >= 0) & (me + o < count)

    def greet(k, carry):
        pl.semaphore_signal(barrier, inc=1, device_id=device(peer(k)), device_id_type=MESH)
        return carry

    lax.fori_loop(1, count, greet, 0)

    def copy(src, dst, send_sem, recv_sem, index):
        return pltpu.make_async_remote_copy(
            src_ref=src, dst_ref=dst, send_sem=send_sem, recv_sem=recv_sem,
            device_id=device(index), device_id_type=MESH,
        )

    def share(src, pool, send, recv):
        def start(k, carry):
            copy(src, pool.at[me], send.at[k], recv.at[me], peer(k)).start()
            return carry

        lax.fori_loop(1, count, start, 0)

    def collect(src, pool, send, recv):
        def wait(k, carry):
            copy(src, pool.at[peer(k)], send.at[k], recv.at[peer(k)], peer(k)).wait()
            return carry

        lax.fori_loop(1, count, wait, 0)

    def spread(src, place, send, recv, offsets):
        for o in offsets:

            @pl.when(exists(o))
            def _():
                copy(src, place(-o), send(o), recv(-o), me + o).start()

    def arrive(src, place, send, recv, offsets):
        for o in offsets:

            @pl.when(exists(o))
            def _():
                copy(src, place(o), send(o), recv(o), me + o).wait()

    def near_spread(e, src):
        args = (src, lambda o: near.at[e, (o + 1) // 2], lambda o: near_send.at[e, (o + 1) // 2],
                lambda o: near_recv.at[e, (o + 1) // 2], (-1, 1))
        spread(*args)
        return lambda: arrive(*args)

    offsets = [sign * o for o in range(1, side + 1) for sign in (-1, 1)]

    evens = [0] + [o for o in offsets if o % 2 == 0]
    odds = [o for o in offsets if o % 2]
    delta = 1 - 2 * (me % 2)

    def direct(e, o):
        return copy(far.at[side], far.at[side - o], far_send.at[e, side + o], far_recv.at[e, side - o], me + o)

    def arrival(e, o):
        return copy(far.at[side], far.at[side + o], far_send.at[e, side + o], far_recv.at[e, side + o], me + o)

    def passed(e, o):
        place = o - delta + side
        return copy(far.at[side + o], far.at[place], far_send.at[e, place], far_recv.at[e, place], me + delta)

    def passes(o):
        return exists(o) & (o - delta >= -side) & (o - delta <= side)

    def far_exchange(e):
        for o in evens[1:]:

            @pl.when(exists(o))
            def _():
                direct(e, o).start()

        for o in evens:
            if o:

                @pl.when(exists(o))
                def _():
                    arrival(e, o).wait_recv()

            @pl.when(passes(o))
            def _():
                passed(e, o).start()

        for o in odds:

            @pl.when(exists(o))
            def _():
                arrival(e, o).wait_recv()

        for o in evens:
            if o:

                @pl.when(exists(o))
                def _():
                    direct(e, o).wait_send()

            @pl.when(passes(o))
            def _():
                passed(e, o).wait_send()

    to_blocks(gradient, xg, tiles)
    for o in (-1, 1):

        @pl.when(jnp.logical_not(exists(o)))
        def _():
            for e in range(near.shape[0]):
                near[e, (o + 1) // 2] = jnp.zeros(near.shape[2:], jnp.float32)
            taps[o + 1] = jnp.zeros(taps.shape[1:], jnp.float32)

    for o in offsets:

        @pl.when(jnp.logical_not(exists(o)))
        def _():
            far[o + side] = jnp.zeros(far.shape[1:], jnp.float32)

    pl.semaphore_wait(barrier, count - 1)
    share(psf, psf_all, psf_send, psf_recv)
    near_done = near_spread(0, xg)
    to_blocks(image, xi, tiles)
    to_blocks(weight, xh, tiles)
    psf_all[me] = psf[...]
    collect(psf, psf_all, psf_send, psf_recv)
    for r in range(8):
        both = psf_all[slot_of[facet[r]]]
        taps[1, r : r + 1, :] = both[0:1]
        flipped[r : r + 1, :] = both[1:2]
    tap_args = (taps.at[1], lambda o: taps.at[o + 1], lambda o: tap_send.at[(o + 1) // 2],
                lambda o: tap_recv.at[(o + 1) // 2], (-1, 1))
    spread(*tap_args)
    arrive(*tap_args)
    build_bases(taps, flipped, base_f, base_a)
    build_weights(base_f, HALF - 1, fh, fl, wide)
    alive = [None if t == side else jnp.where(exists(t - side), 1.0, 0.0) for t in range(2 * side + 1)]

    for sweep in range(SUBITERS):
        if sweep == 0:
            descent = xg
        else:
            descent = middle
            e = 3 * sweep - 2
            done = near_spread(e, current_change)
            done()
            change = current_change[...]
            pushed = xh[...] * blur([near[e, 0], change, near[e, 1]], fh, fl)
            far[side] = pushed
            near_done = near_spread(e + 1, far.at[side])
            near_done()
            middle[...] = xg[...] + blur([near[e + 1, 0], pushed, near[e + 1, 1]], ah, al)
            near_done = near_spread(e + 2, middle)
        near_done()
        e = 3 * sweep
        d = descent[...]
        b = blur([near[e, 0], d, near[e, 1]], fh, fl)

        def lanes(x):
            column = jnp.sum(x, axis=0, keepdims=True)
            return column[:, :LANES] + column[:, LANES:]

        sums[sweep, me] = jnp.concatenate([lanes(d * d), lanes(xh[...] * b * b)], axis=0)
        own = sums.at[sweep, me]
        share(own, sums.at[sweep], sum_send.at[sweep], sum_recv.at[sweep])
        if sweep == 0:
            build_weights(base_a, HALF, ah, al, wide)
        collect(own, sums.at[sweep], sum_send.at[sweep], sum_recv.at[sweep])
        totals = jnp.sum(jnp.sum(sums[sweep], axis=0), axis=1, keepdims=True)
        step = totals[0:1] / totals[1:2]
        start = xi if sweep == 0 else current
        far[side] = start[...] - step * d
        far_exchange(sweep)
        stripes = [far.at[t] for t in range(2 * side + 1)]
        column_cascade(stripes, alive, levels, 8)
        row_cascade(levels, spline)
        new = keep(far[side], levels, [step * thresholds[k] for k in range(levels.shape[0])])
        current[...] = new
        if sweep < SUBITERS - 1:
            current_change = far.at[side]
            current_change[...] = new - xi[...]
    from_blocks(current, out, tiles)


MESH = pl.DeviceIdType.MESH


def stripe_body(image_now, gradient, hessian_weight, psf_tiles, facet_of_row, tile_slot, thresholds):
    band, columns = image_now.shape
    levels = thresholds.shape[0]
    blocks = columns // BLOCK
    scales = lax.axis_size("scales")
    count = lax.axis_size("rows") * scales
    reach = 2 ** (levels + 1) - 2
    side = -(-reach // band)
    own = psf_tiles.reshape(TILE, TILE)
    psf = jnp.stack([own, jnp.flip(own, axis=1)]).reshape(2, TILE * TILE)
    plane = (blocks, WIDTH)
    table = pltpu.VMEM((6, WIDTH, WIDTH), jnp.bfloat16)
    f32 = lambda *shape: pltpu.VMEM(shape, jnp.float32)
    sem = lambda *shape: pltpu.SemaphoreType.DMA(shape)
    smem = pl.BlockSpec(memory_space=pltpu.SMEM)
    exchanges = 3 * SUBITERS - 2
    return pl.pallas_call(
        functools.partial(stripe_kernel, count, scales, side),
        out_shape=jax.ShapeDtypeStruct((band, columns), jnp.float32),
        in_specs=[VMEM] * 4 + [smem] * 3 + [VMEM],
        out_specs=VMEM,
        scratch_shapes=[
            f32(*plane), f32(*plane), f32(*plane), f32(*plane),
            f32(exchanges, 2, *plane), f32(*plane), f32(2 * side + 1, *plane),
            f32(count, 2, TILE * TILE), f32(3, 8, TILE * TILE), f32(8, TILE * TILE),
            f32(3 * band, WIDTH), f32(3 * band, WIDTH), table, table, table, table,
            f32(levels, *plane), f32(SUBITERS, count, 2, LANES),
            f32(columns // LANES * 8, LANES), f32(2, 2, WIDTH, LANES),
            sem(count), sem(count), sem(SUBITERS, count), sem(SUBITERS, count), sem(2), sem(2),
            sem(exchanges, 2), sem(exchanges, 2),
            sem(SUBITERS, 2 * side + 1), sem(SUBITERS, 2 * side + 1),
        ],
        compiler_params=pltpu.CompilerParams(
            collective_id=0, has_side_effects=True, vmem_limit_bytes=56 * 1024 * 1024
        ),
    )(image_now, gradient, hessian_weight, psf, facet_of_row, tile_slot, thresholds, spline_matrices(levels))


EDGE = 80
BASE = EDGE + 8
WEIGHT_EDGE = 40
PARTS = 2
HEIGHT = PARTS * LANES


def wide(ref, start, n):
    return jnp.concatenate([ref[p, pl.ds(start, n), :] for p in range(PARTS)], axis=1)


def put(ref, start, x):
    for p in range(PARTS):
        ref[p, pl.ds(start, x.shape[0]), :] = x[:, p * LANES : (p + 1) * LANES]


def iotas(shape):
    return lax.broadcasted_iota(jnp.int32, shape, 0), lax.broadcasted_iota(jnp.int32, shape, 1)


def build_splines(splines):
    i, j = iotas((HEIGHT, HEIGHT))
    o = jnp.abs(i - j)
    for level in range(splines.shape[0]):
        d = 2**level
        coef = jnp.where(o == 0, 0.375, jnp.where(o == d, 0.25, jnp.where(o == 2 * d, 0.0625, 0.0)))
        splines[level] = coef.astype(jnp.bfloat16)


def gather_taps(pool, turned, band, taps, taps_t):
    count = pool.shape[0]
    tile = jnp.concatenate([pool[:, 0, :], pool[:, 1, :]], axis=1)
    for n in range(TILE):
        shift = TILE * (n - HALF) % (TILE * TILE)
        turned[n * count : (n + 1) * count, :] = pltpu.roll(tile, shift, 1) if shift else tile
    row, lane = iotas((HEIGHT, count))
    spread = jnp.where(row // band == lane, 1.0, 0.0).astype(jnp.bfloat16)
    row, lane = iotas((HEIGHT, LANES))
    slots = dot(spread, pool[:, 2, :].astype(jnp.bfloat16))
    slot = jnp.sum(jnp.where(lane == row % band, slots, 0.0), axis=1, keepdims=True)
    row, lane = iotas((HEIGHT, TILE * count))
    chosen = (slot == (lane % count).astype(jnp.float32)) & (row % TILE == lane // count)
    chosen = jnp.where(chosen, 1.0, 0.0).astype(jnp.bfloat16)
    for n, part in enumerate(halves(turned[...])):
        x = dot(chosen, part)
        taps[n] = x
        taps_t[n] = x.T


def build_forward(taps_t, tables):
    row, lane = iotas((HEIGHT, TILE * TILE))
    repeat = jnp.where(row % TILE == lane // TILE, 1.0, 0.0).astype(jnp.bfloat16)
    r, c = iotas((HEIGHT, HEIGHT))
    inside = (r - c + HALF >= 0) & (r - c + HALF < TILE)
    row, _ = iotas((TILE * TILE, HEIGHT))

    def one(b, carry):
        rows = pl.ds(pl.multiple_of(b * HEIGHT, HEIGHT), HEIGHT)
        for n in range(2):
            x = jnp.where(row % TILE == b, taps_t[n], 0.0).astype(jnp.bfloat16)
            tables[n, rows, :] = jnp.where(inside, dot(repeat, x), 0.0).astype(jnp.bfloat16)
        return carry

    lax.fori_loop(0, TILE, one, 0)


def build_adjoint(taps, tables):
    row, lane = iotas((TILE * TILE, HEIGHT))
    repeat = jnp.where(lane % TILE == row // TILE, 1.0, 0.0).astype(jnp.bfloat16)
    r, c = iotas((HEIGHT, HEIGHT))
    inside = (c - r + HALF >= 0) & (c - r + HALF < TILE)
    _, lane = iotas((HEIGHT, TILE * TILE))

    def one(b, carry):
        rows = pl.ds(pl.multiple_of(b * HEIGHT, HEIGHT), HEIGHT)
        for n in range(2):
            x = jnp.where(lane % TILE == b, taps[n], 0.0).astype(jnp.bfloat16)
            tables[n, rows, :] = jnp.where(inside, dot(x, repeat), 0.0).astype(jnp.bfloat16)
        return carry

    lax.fori_loop(0, TILE, one, 0)


def tile_blur(src, low, n, tables, sign, high_ref, low_ref):
    rows = pl.ds(0, n)
    for b in range(TILE):
        high, rest = halves(wide(src, BASE + low + sign * (b - HALF), n))
        high_ref[rows, b * HEIGHT : (b + 1) * HEIGHT] = high
        low_ref[rows, b * HEIGHT : (b + 1) * HEIGHT] = rest
    high = high_ref[rows, :]
    return dot(high, tables[0]) + dot(low_ref[rows, :], tables[0]) + dot(high, tables[1])


def cascade(src, levels_ref, splines, width, reaches, alive):
    for level, reach in enumerate(reaches):
        d = 2**level
        source = src if level == 0 else levels_ref.at[level - 1]
        sides = []
        for p in range(PARTS):

            def smooth(start, n):
                x = lambda o: source[p, pl.ds(BASE + start + o, n), :]
                return 0.0625 * (x(-2 * d) + x(2 * d)) + 0.25 * (x(-d) + x(d)) + 0.375 * x(0)

            own = smooth(0, width)
            if reach:
                own = jnp.concatenate(
                    [smooth(-reach, reach) * alive[0], own, smooth(width, reach) * alive[1]], axis=0
                )
            sides.append(own)
        high, low = halves(jnp.concatenate(sides, axis=1))
        put(levels_ref.at[level], BASE - reach, dot(high, splines[level]) + dot(low, splines[level]))


def thresholded(planes, moves, step, limits, p, rows):
    def level(k):
        return planes[k][p, rows, :] - step * moves[k][p, rows, :]

    smooth = level(0)
    total = None
    for k, limit in enumerate(limits):
        smoother = level(k + 1)
        detail = smooth - smoother
        part = detail - jnp.clip(detail, -limit, limit)
        total = part if total is None else total + part
        smooth = smoother
    return total + smooth


def tile_kernel(
    row_count, scales,
    image, gradient, weight, psf, facet, slot_of, thresholds,
    out,
    landed, g, x, h, new, change, pushed, descent, x_levels, d_levels, splines,
    pack, pool, turned, taps, taps_t, forward, adjoint, high, low, blurred, sums, result,
    psf_send, psf_recv, move_send, move_recv, edge_send, edge_recv, sum_send, sum_recv, out_send, out_recv,
):
    count = row_count * scales
    band = image.shape[0]
    width = image.shape[1] // count
    levels = thresholds.shape[0]
    snake = row_count % 2 == 0 and scales % 2 == 0
    me = lax.axis_index("rows") * scales + lax.axis_index("scales")
    barrier = pltpu.get_barrier_semaphore()

    def device(index):
        return (index // scales, index % scales)

    def place(index):
        if not snake:
            return index
        r, s = index // scales, index % scales
        z, flat = r // 2, r % 2
        line = 2 * z + flat + (z % 2) * (1 - 2 * flat)
        y = s // 2
        y = y + (line % 2) * (scales // 2 - 1 - 2 * y)
        return (line * (scales // 2) + y) * 2 + s % 2

    def holder(position):
        if not snake:
            return position
        chip = position // 2
        line, y = chip // (scales // 2), chip % (scales // 2)
        y = y + (line % 2) * (scales // 2 - 1 - 2 * y)
        z, flat = line // 2, line % 2
        flat = flat + (z % 2) * (1 - 2 * flat)
        return (2 * z + flat) * scales + 2 * y + position % 2

    here = place(me)

    def peer(k):
        return (me + k) % count

    def columns(index):
        return pl.ds(pl.multiple_of(width * index, LANES), width)

    def stripe(index):
        return pl.ds(pl.multiple_of(band * index, band), band)

    def greet(k, carry):
        pl.semaphore_signal(barrier, inc=1, device_id=device(peer(k)), device_id_type=MESH)
        return carry

    lax.fori_loop(1, count, greet, 0)

    def copy(src, dst, send_sem, recv_sem, index):
        return pltpu.make_async_remote_copy(
            src_ref=src, dst_ref=dst, send_sem=send_sem, recv_sem=recv_sem,
            device_id=device(index), device_id_type=MESH,
        )

    def share(src, dst, send, recv):
        def start(k, carry):
            p = peer(k)
            copy(src(p), dst, send, recv, p).start()
            return carry

        lax.fori_loop(1, count, start, 0)

    def all_of(ref, send, recv):
        return copy(ref, ref, send, recv, peer(1))

    def edges(n, ref, reach):
        right = copy(ref.at[:, pl.ds(BASE + width - reach, reach)], ref.at[:, pl.ds(BASE - reach, reach)],
                     edge_send.at[n, 0], edge_recv.at[n, 0], holder((here + 1) % count))
        left = copy(ref.at[:, pl.ds(BASE, reach)], ref.at[:, pl.ds(BASE + width, reach)],
                    edge_send.at[n, 1], edge_recv.at[n, 1], holder((here + count - 1) % count))

        def start():
            @pl.when(here > 0)
            def _():
                left.start()

            @pl.when(here < count - 1)
            def _():
                right.start()

        def arrive():
            @pl.when(here > 0)
            def _():
                left.wait_send()
                right.wait_recv()

            @pl.when(here < count - 1)
            def _():
                right.wait_send()
                left.wait_recv()

        return start, arrive

    lane = lax.broadcasted_iota(jnp.int32, (1, LANES), 1)
    slots = jnp.zeros((1, LANES), jnp.float32)
    for r in range(band):
        slots = jnp.where(lane == r, slot_of[facet[r]].astype(jnp.float32), slots)
    pack[0:1, :] = psf[:, :LANES]
    pack[1:2, :] = psf[:, LANES:]
    pack[2:3, :] = slots
    pool[me] = pack[...]
    moving = [gradient, image, weight]
    for n, source in enumerate(moving):
        landed[n, stripe(me), :] = source[:, columns(here)]
    for ref in (g, x, descent):
        for p in range(PARTS):
            ref[p, pl.ds(0, BASE), :] = jnp.zeros((BASE, LANES), jnp.float32)
            ref[p, pl.ds(BASE + width, BASE), :] = jnp.zeros((BASE, LANES), jnp.float32)
    for p in range(PARTS):
        h[p, pl.ds(BASE - WEIGHT_EDGE, WEIGHT_EDGE), :] = jnp.zeros((WEIGHT_EDGE, LANES), jnp.float32)
        h[p, pl.ds(BASE + width, WEIGHT_EDGE), :] = jnp.zeros((WEIGHT_EDGE, LANES), jnp.float32)
    build_splines(splines)
    alive = [jnp.where(here > 0, 1.0, 0.0), jnp.where(here < count - 1, 1.0, 0.0)]

    pl.semaphore_wait(barrier, count - 1)
    share(lambda p: pack, pool.at[me], psf_send.at[0], psf_recv.at[0])
    for n, source in enumerate(moving):
        share(lambda p: source.at[:, columns(place(p))], landed.at[n, stripe(me)], move_send.at[n], move_recv.at[n])

    others = pl.ds(0, count - 1)
    others_rows = pl.ds(0, (count - 1) * band)

    def arrived(n, ref):
        all_of(landed.at[n, others_rows], move_send.at[n], move_recv.at[n]).wait_recv()
        put(ref, BASE, landed[n].T)

    all_of(pool.at[others], psf_send.at[0], psf_recv.at[0]).wait()
    gather_taps(pool, turned, band, taps, taps_t)
    build_forward(taps_t, forward)
    arrived(0, g)
    start, arrive = edges(0, g, EDGE)
    start()
    build_adjoint(taps, adjoint)
    arrive()
    blurred[...] = tile_blur(g, 0, width, forward, 1, high, low)
    outer = (80, 72, 64, 48)
    inner = (32, 24, 16, 0)
    cascade(g, d_levels, splines, width, outer, alive)
    arrived(1, x)
    start, arrive = edges(1, x, EDGE)
    start()
    arrive()
    cascade(x, x_levels, splines, width, outer, alive)
    arrived(2, h)
    weight_start, weight_arrive = edges(2, h, WEIGHT_EDGE)
    weight_start()

    def share_sums(sweep, moved):
        d, b, w = wide(moved, BASE, width), blurred[...], wide(h, BASE, width)

        def lanes(values):
            column = jnp.sum(values, axis=0, keepdims=True)
            return column[:, :LANES] + column[:, LANES:]

        sums[sweep, me] = jnp.concatenate([lanes(d * d), lanes(w * b * b)], axis=0)
        share(lambda p: sums.at[sweep, me], sums.at[sweep, me], sum_send.at[sweep], sum_recv.at[sweep])

    def step_of(sweep):
        all_of(sums.at[sweep, others], sum_send.at[sweep], sum_recv.at[sweep]).wait()
        totals = jnp.sum(jnp.sum(sums[sweep], axis=0), axis=1, keepdims=True)
        return totals[0:1] / totals[1:2]

    def chunks(reach):
        return [pl.ds(BASE - reach + n, 32) for n in range(0, width + 2 * reach, 32)]

    share_sums(0, g)
    step = step_of(0)
    limits = [step * thresholds[k] for k in range(levels)]
    planes = [x] + [x_levels.at[k] for k in range(levels)]
    moves = [g] + [d_levels.at[k] for k in range(levels)]
    for rows in chunks(outer[-1]):
        for p in range(PARTS):
            value = thresholded(planes, moves, step, limits, p, rows)
            new[p, rows, :] = value
            change[p, rows, :] = value - x[p, rows, :]
    weight_arrive()
    n = width + 2 * WEIGHT_EDGE
    value = tile_blur(change, -WEIGHT_EDGE, n, forward, 1, high, low)
    put(pushed, BASE - WEIGHT_EDGE, value * wide(h, BASE - WEIGHT_EDGE, n))
    reach = inner[0]
    n = width + 2 * reach
    value = tile_blur(pushed, -reach, n, adjoint, -1, high, low) + wide(g, BASE - reach, n)
    value = jnp.concatenate(
        [value[:reach] * alive[0], value[reach : reach + width], value[reach + width :] * alive[1]], axis=0
    )
    put(descent, BASE - reach, value)
    blurred[...] = tile_blur(descent, 0, width, forward, 1, high, low)
    share_sums(1, descent)
    cascade(new, x_levels, splines, width, inner, alive)
    cascade(descent, d_levels, splines, width, inner, alive)
    step = step_of(1)
    limits = [step * thresholds[k] for k in range(levels)]
    planes[0], moves[0] = new, descent
    for rows in chunks(0):
        for p in range(PARTS):
            change[p, rows, :] = thresholded(planes, moves, step, limits, p, rows)
    result[...] = wide(change, BASE, width).T
    share(lambda p: result.at[stripe(p)], out.at[:, columns(here)], out_send.at[0], out_recv.at[0])
    out[:, columns(here)] = result[stripe(me), :]
    for n in range(len(moving)):
        all_of(landed.at[n, others_rows], move_send.at[n], move_recv.at[n]).wait_send()
    all_of(result.at[others_rows], out_send.at[0], out_recv.at[0]).wait_send()
    all_of(out.at[:, pl.ds(0, (count - 1) * width)], out_send.at[0], out_recv.at[0]).wait_recv()


def tile_body(image_now, gradient, hessian_weight, psf_tiles, facet_of_row, tile_slot, thresholds):
    band, columns = image_now.shape
    levels = thresholds.shape[0]
    rows, scales = lax.axis_size("rows"), lax.axis_size("scales")
    count = rows * scales
    width = columns // count
    f32 = lambda *shape: pltpu.VMEM(shape, jnp.float32)
    b16 = lambda *shape: pltpu.VMEM(shape, jnp.bfloat16)
    sem = lambda *shape: pltpu.SemaphoreType.DMA(shape)
    smem = pl.BlockSpec(memory_space=pltpu.SMEM)
    plane = (PARTS, width + 2 * BASE, LANES)
    table = b16(2, TILE * HEIGHT, HEIGHT)
    lined = b16(width + 2 * EDGE, TILE * HEIGHT)
    return pl.pallas_call(
        functools.partial(tile_kernel, rows, scales),
        out_shape=jax.ShapeDtypeStruct((band, columns), jnp.float32),
        in_specs=[VMEM] * 4 + [smem] * 3,
        out_specs=VMEM,
        scratch_shapes=[
            f32(3, HEIGHT, width), *[f32(*plane)] * 7, f32(levels, *plane), f32(levels, *plane),
            b16(levels, HEIGHT, HEIGHT),
            f32(3, LANES), f32(count, 3, LANES), f32(TILE * count, TILE * TILE),
            f32(2, HEIGHT, TILE * TILE), f32(2, TILE * TILE, HEIGHT), table, table, lined, lined,
            f32(width, HEIGHT), f32(SUBITERS, count, 2, LANES), f32(HEIGHT, width),
            sem(1), sem(1), sem(3), sem(3), sem(3, 2), sem(3, 2), sem(SUBITERS), sem(SUBITERS), sem(1), sem(1),
        ],
        compiler_params=pltpu.CompilerParams(
            collective_id=0, has_side_effects=True, vmem_limit_bytes=56 * 1024 * 1024
        ),
    )(image_now, gradient, hessian_weight, psf_tiles, facet_of_row, tile_slot, thresholds)


def body(image_now, *rest):
    band, columns = image_now.shape
    count = lax.axis_size("rows") * lax.axis_size("scales")
    levels = rest[-1].shape[0]
    whole = columns % (count * LANES) == 0 and columns // count >= LANES and band * count == HEIGHT and levels == 4
    return (tile_body if whole else stripe_body)(image_now, *rest)


def solution(mesh):
    band = P(AXES, None)
    in_specs = (band, band, band, band, P(AXES), P(), P())
    return jax.shard_map(body, mesh=mesh, in_specs=in_specs, out_specs=band, check_vma=False)
```

```python
import functools

import jax
import jax.numpy as jnp
import numpy as np
from jax import lax
from jax.experimental import pallas as pl
from jax.experimental.pallas import tpu as pltpu
from jax.sharding import PartitionSpec as P

TILE = 16
HALF = TILE // 2
SUBITERS = 2
LANES = 128
BLOCK = 32
GROUPS = LANES // BLOCK
WIDTH = 8 * BLOCK
AXES = ("rows", "scales")
VMEM = pl.BlockSpec(memory_space=pltpu.VMEM)


def spline_matrices(levels):
    w = np.arange(WIDTH)
    same = (w[:, None] // BLOCK) == (w[None, :] // BLOCK)
    place = w % BLOCK
    nearer = place + np.where(place < BLOCK // 2, BLOCK, -BLOCK)
    planes = []
    for level in range(levels):
        d = 2**level
        for column in (place, nearer):
            o = np.abs(column[:, None] - place[None, :])
            coef = np.where(o == 0, 0.375, np.where(o == d, 0.25, np.where(o == 2 * d, 0.0625, 0.0)))
            planes.append(np.where(same, coef, 0.0))
    return jnp.asarray(np.stack(planes), jnp.bfloat16)


def halves(x):
    high = x.astype(jnp.bfloat16)
    low = (x - high.astype(jnp.float32)).astype(jnp.bfloat16)
    return high, low


def dot(a, b):
    return jnp.dot(a, b, preferred_element_type=jnp.float32)


def block_shift(x, s):
    if s == 0:
        return x
    count = x.shape[0] // GROUPS
    parts = [x[p * count : (p + 1) * count] for p in range(GROUPS)]
    row = lax.broadcasted_iota(jnp.int32, parts[0].shape, 0)
    if s == 1:
        last = jnp.where(row == count - 1, 0.0, pltpu.roll(parts[0], count - 1, 0))
        return jnp.concatenate(parts[1:] + [last], axis=0)
    first = jnp.where(row == 0, 0.0, pltpu.roll(parts[-1], 1, 0))
    return jnp.concatenate([first] + parts[:-1], axis=0)


def beside(x):
    lane = lax.broadcasted_iota(jnp.int32, x.shape, 1) % BLOCK
    return jnp.where(lane < BLOCK // 2, block_shift(x, 1), block_shift(x, -1))


def blur(stripes, high_ref, low_ref):
    total = None
    for t, x in enumerate(stripes):
        for n, y in enumerate((x, beside(x))):
            high, low = halves(y)
            w = high_ref[t * 2 + n]
            part = dot(high, w) + dot(low, w) + dot(high, low_ref[t * 2 + n])
            total = part if total is None else total + part
    return total


def to_blocks(src_ref, dst_ref, tiles):
    count = src_ref.shape[1] // LANES
    for q in range(count):
        tiles[pl.ds(8 * q, 8), :] = src_ref[:, q * LANES : (q + 1) * LANES]
    group = lax.broadcasted_iota(jnp.int32, (count, LANES), 1) // BLOCK
    for half in range(2):
        outs = [None] * GROUPS
        for k in range(4):
            a = tiles[pl.ds(half * 4 + k, count, stride=8), :]
            for p in range(GROUPS):
                shift = BLOCK * ((k - p) % 4)
                moved = pltpu.roll(a, shift, 1) if shift else a
                outs[p] = moved if k == 0 else jnp.where(group == k, moved, outs[p])
        for p in range(GROUPS):
            dst_ref[p * count : (p + 1) * count, half * LANES : (half + 1) * LANES] = outs[p]


def from_blocks(src_ref, dst_ref, tiles):
    count = dst_ref.shape[1] // LANES
    group = lax.broadcasted_iota(jnp.int32, (count, LANES), 1) // BLOCK
    for half in range(2):
        for k in range(4):
            out = None
            for p in range(GROUPS):
                x = src_ref[p * count : (p + 1) * count, half * LANES : (half + 1) * LANES]
                shift = BLOCK * ((p - k) % 4)
                moved = pltpu.roll(x, shift, 1) if shift else x
                out = moved if p == 0 else jnp.where(group == p, moved, out)
            tiles[pl.ds(half * 4 + k, count, stride=8), :] = out
    for q in range(count):
        dst_ref[:, q * LANES : (q + 1) * LANES] = tiles[pl.ds(8 * q, 8), :]


def build_weights(base_ref, lead, high_ref, low_ref, wide):
    lane = lax.broadcasted_iota(jnp.int32, (8, WIDTH), 1) % BLOCK
    for t in range(3):
        base = base_ref[8 * t : 8 * t + 8, :]
        for w in range(BLOCK):
            for n, s in enumerate((0, 1 if w < BLOCK // 2 else -1)):
                moved = pltpu.roll(base, (w - lead + BLOCK * s) % WIDTH, 1)
                x = lane - (w - lead + BLOCK * s)
                kept = jnp.where((x >= 0) & (x < TILE), moved, 0.0)
                for half in range(2):
                    wide[n, half, pl.ds(w, 8, stride=BLOCK), :] = kept[
                        :, half * LANES : (half + 1) * LANES
                    ]
        for n in range(2):
            for half in range(2):
                high, low = halves(wide[n, half])
                high_ref[t * 2 + n, :, half * LANES : (half + 1) * LANES] = high
                low_ref[t * 2 + n, :, half * LANES : (half + 1) * LANES] = low


def moved_rows(vregs, rolls, i, d):
    if d % 4 == 0:
        return vregs[i + d // 4]
    shift = (-BLOCK * d) % LANES

    def rolled(n):
        if (n, shift) not in rolls:
            rolls[(n, shift)] = pltpu.roll(vregs[n], shift, 1)
        return rolls[(n, shift)]

    lane = lax.broadcasted_iota(jnp.int32, vregs[i].shape, 1)
    if d > 0:
        return jnp.where(lane < LANES - BLOCK * d, rolled(i), rolled(i + 1))
    return jnp.where(lane >= -BLOCK * d, rolled(i), rolled(i - 1))


def column_cascade(stripe_refs, alive, levels_ref, step_rows):
    reach = len(stripe_refs) // 2
    levels = levels_ref.shape[0]

    def chunk(n, carry):
        rows = pl.ds(pl.multiple_of(n * step_rows, step_rows), step_rows)
        vregs = {}
        for t, ref in enumerate(stripe_refs):
            for half in range(2):
                vregs[2 * t + half] = ref[rows, half * LANES : (half + 1) * LANES]
        own = 2 * reach
        for level in range(levels):
            d = 2**level
            left = 2 ** (levels + 1) - 2 ** (level + 2)
            margin = -(-left // 4)
            rolls, out = {}, {}
            keys = vregs
            for i in range(own - margin, own + 2 + margin):
                outer = moved_rows(keys, rolls, i, -2 * d) + moved_rows(keys, rolls, i, 2 * d)
                inner = moved_rows(keys, rolls, i, -d) + moved_rows(keys, rolls, i, d)
                value = 0.0625 * outer + 0.25 * inner + 0.375 * keys[i]
                t = i // 2
                out[i] = value if t == reach else value * alive[t]
            vregs = out
            for half in range(2):
                levels_ref[level, rows, half * LANES : (half + 1) * LANES] = out[own + half]
        return carry

    lax.fori_loop(0, stripe_refs[0].shape[0] // step_rows, chunk, 0)


def row_cascade(levels_ref, spline_ref):
    levels = levels_ref.shape[0]
    for level in range(levels):

        def one(k, carry):
            x = levels_ref[k]
            total = None
            for n, y in enumerate((x, beside(x))):
                high, low = halves(y)
                w = spline_ref[level * 2 + n]
                part = dot(high, w) + dot(low, w)
                total = part if total is None else total + part
            levels_ref[k] = total
            return carry

        lax.fori_loop(level, levels, one, 0)


def keep(own, levels_ref, limits):
    levels = levels_ref.shape[0]
    smooth = own
    total = None
    for k in range(levels):
        smoother = levels_ref[k]
        detail = smooth - smoother
        part = detail - jnp.clip(detail, -limits[k], limits[k])
        total = part if total is None else total + part
        smooth = smoother
    return total + smooth


def build_bases(taps, flipped, forward, adjoint):
    lane = lax.broadcasted_iota(jnp.int32, (8, WIDTH), 1)
    sub = lax.broadcasted_iota(jnp.int32, (8, WIDTH), 0)
    group, inside = lane // BLOCK, lane % BLOCK < TILE
    own = flipped[...]
    turned = [pltpu.roll(own, TILE * n, 1) if n else own for n in range(TILE)]
    forward[...] = jnp.zeros_like(forward)
    for a in range(TILE):
        placed = jnp.zeros((8, WIDTH), jnp.float32)
        for r in range(8):
            placed = jnp.where((sub == r) & (group == r) & inside, turned[(2 * r - a) % TILE], placed)
        forward[a : a + 8, :] += placed
    for t in range(3):
        x = taps[t]
        row = sub + 8 * t
        tap = group - row + TILE
        placed = jnp.zeros((8, WIDTH), jnp.float32)
        for n in range(TILE):
            moved = pltpu.roll(x, TILE * n, 1) if n else x
            use = ((group + row) % TILE == n) & inside & (tap >= 0) & (tap < TILE)
            placed = jnp.where(use, moved, placed)
        adjoint[8 * t : 8 * t + 8, :] = placed


def stripe_kernel(
    count, scales, side,
    image, gradient, weight, psf, facet, slot_of, thresholds, spline,
    out,
    xi, xg, xh, current, near, middle, far, psf_all, taps, flipped, base_f, base_a, fh, fl, ah, al,
    levels, sums, tiles, wide,
    psf_send, psf_recv, sum_send, sum_recv, tap_send, tap_recv, near_send, near_recv, far_send, far_recv,
):
    me = lax.axis_index("rows") * scales + lax.axis_index("scales")
    barrier = pltpu.get_barrier_semaphore()

    def device(index):
        return (index // scales, index % scales)

    def peer(k):
        return (me + k) % count

    def exists(o):
        return (me + o >= 0) & (me + o < count)

    def greet(k, carry):
        pl.semaphore_signal(barrier, inc=1, device_id=device(peer(k)), device_id_type=MESH)
        return carry

    lax.fori_loop(1, count, greet, 0)

    def copy(src, dst, send_sem, recv_sem, index):
        return pltpu.make_async_remote_copy(
            src_ref=src, dst_ref=dst, send_sem=send_sem, recv_sem=recv_sem,
            device_id=device(index), device_id_type=MESH,
        )

    def share(src, pool, send, recv):
        def start(k, carry):
            copy(src, pool.at[me], send.at[k], recv.at[me], peer(k)).start()
            return carry

        lax.fori_loop(1, count, start, 0)

    def collect(src, pool, send, recv):
        def wait(k, carry):
            copy(src, pool.at[peer(k)], send.at[k], recv.at[peer(k)], peer(k)).wait()
            return carry

        lax.fori_loop(1, count, wait, 0)

    def spread(src, place, send, recv, offsets):
        for o in offsets:

            @pl.when(exists(o))
            def _():
                copy(src, place(-o), send(o), recv(-o), me + o).start()

    def arrive(src, place, send, recv, offsets):
        for o in offsets:

            @pl.when(exists(o))
            def _():
                copy(src, place(o), send(o), recv(o), me + o).wait()

    def near_spread(e, src):
        args = (src, lambda o: near.at[e, (o + 1) // 2], lambda o: near_send.at[e, (o + 1) // 2],
                lambda o: near_recv.at[e, (o + 1) // 2], (-1, 1))
        spread(*args)
        return lambda: arrive(*args)

    offsets = [sign * o for o in range(1, side + 1) for sign in (-1, 1)]

    evens = [0] + [o for o in offsets if o % 2 == 0]
    odds = [o for o in offsets if o % 2]
    delta = 1 - 2 * (me % 2)

    def direct(e, o):
        return copy(far.at[side], far.at[side - o], far_send.at[e, side + o], far_recv.at[e, side - o], me + o)

    def arrival(e, o):
        return copy(far.at[side], far.at[side + o], far_send.at[e, side + o], far_recv.at[e, side + o], me + o)

    def passed(e, o):
        place = o - delta + side
        return copy(far.at[side + o], far.at[place], far_send.at[e, place], far_recv.at[e, place], me + delta)

    def passes(o):
        return exists(o) & (o - delta >= -side) & (o - delta <= side)

    def far_exchange(e):
        for o in evens[1:]:

            @pl.when(exists(o))
            def _():
                direct(e, o).start()

        for o in evens:
            if o:

                @pl.when(exists(o))
                def _():
                    arrival(e, o).wait_recv()

            @pl.when(passes(o))
            def _():
                passed(e, o).start()

        for o in odds:

            @pl.when(exists(o))
            def _():
                arrival(e, o).wait_recv()

        for o in evens:
            if o:

                @pl.when(exists(o))
                def _():
                    direct(e, o).wait_send()

            @pl.when(passes(o))
            def _():
                passed(e, o).wait_send()

    to_blocks(gradient, xg, tiles)
    for o in (-1, 1):

        @pl.when(jnp.logical_not(exists(o)))
        def _():
            for e in range(near.shape[0]):
                near[e, (o + 1) // 2] = jnp.zeros(near.shape[2:], jnp.float32)
            taps[o + 1] = jnp.zeros(taps.shape[1:], jnp.float32)

    for o in offsets:

        @pl.when(jnp.logical_not(exists(o)))
        def _():
            far[o + side] = jnp.zeros(far.shape[1:], jnp.float32)

    pl.semaphore_wait(barrier, count - 1)
    share(psf, psf_all, psf_send, psf_recv)
    near_done = near_spread(0, xg)
    to_blocks(image, xi, tiles)
    to_blocks(weight, xh, tiles)
    psf_all[me] = psf[...]
    collect(psf, psf_all, psf_send, psf_recv)
    for r in range(8):
        both = psf_all[slot_of[facet[r]]]
        taps[1, r : r + 1, :] = both[0:1]
        flipped[r : r + 1, :] = both[1:2]
    tap_args = (taps.at[1], lambda o: taps.at[o + 1], lambda o: tap_send.at[(o + 1) // 2],
                lambda o: tap_recv.at[(o + 1) // 2], (-1, 1))
    spread(*tap_args)
    arrive(*tap_args)
    build_bases(taps, flipped, base_f, base_a)
    build_weights(base_f, HALF - 1, fh, fl, wide)
    alive = [None if t == side else jnp.where(exists(t - side), 1.0, 0.0) for t in range(2 * side + 1)]

    for sweep in range(SUBITERS):
        if sweep == 0:
            descent = xg
        else:
            descent = middle
            e = 3 * sweep - 2
            done = near_spread(e, current_change)
            done()
            change = current_change[...]
            pushed = xh[...] * blur([near[e, 0], change, near[e, 1]], fh, fl)
            far[side] = pushed
            near_done = near_spread(e + 1, far.at[side])
            near_done()
            middle[...] = xg[...] + blur([near[e + 1, 0], pushed, near[e + 1, 1]], ah, al)
            near_done = near_spread(e + 2, middle)
        near_done()
        e = 3 * sweep
        d = descent[...]
        b = blur([near[e, 0], d, near[e, 1]], fh, fl)

        def lanes(x):
            column = jnp.sum(x, axis=0, keepdims=True)
            return column[:, :LANES] + column[:, LANES:]

        sums[sweep, me] = jnp.concatenate([lanes(d * d), lanes(xh[...] * b * b)], axis=0)
        own = sums.at[sweep, me]
        share(own, sums.at[sweep], sum_send.at[sweep], sum_recv.at[sweep])
        if sweep == 0:
            build_weights(base_a, HALF, ah, al, wide)
        collect(own, sums.at[sweep], sum_send.at[sweep], sum_recv.at[sweep])
        totals = jnp.sum(jnp.sum(sums[sweep], axis=0), axis=1, keepdims=True)
        step = totals[0:1] / totals[1:2]
        start = xi if sweep == 0 else current
        far[side] = start[...] - step * d
        far_exchange(sweep)
        stripes = [far.at[t] for t in range(2 * side + 1)]
        column_cascade(stripes, alive, levels, 8)
        row_cascade(levels, spline)
        new = keep(far[side], levels, [step * thresholds[k] for k in range(levels.shape[0])])
        current[...] = new
        if sweep < SUBITERS - 1:
            current_change = far.at[side]
            current_change[...] = new - xi[...]
    from_blocks(current, out, tiles)


MESH = pl.DeviceIdType.MESH


def stripe_body(image_now, gradient, hessian_weight, psf_tiles, facet_of_row, tile_slot, thresholds):
    band, columns = image_now.shape
    levels = thresholds.shape[0]
    blocks = columns // BLOCK
    scales = lax.axis_size("scales")
    count = lax.axis_size("rows") * scales
    reach = 2 ** (levels + 1) - 2
    side = -(-reach // band)
    own = psf_tiles.reshape(TILE, TILE)
    psf = jnp.stack([own, jnp.flip(own, axis=1)]).reshape(2, TILE * TILE)
    plane = (blocks, WIDTH)
    table = pltpu.VMEM((6, WIDTH, WIDTH), jnp.bfloat16)
    f32 = lambda *shape: pltpu.VMEM(shape, jnp.float32)
    sem = lambda *shape: pltpu.SemaphoreType.DMA(shape)
    smem = pl.BlockSpec(memory_space=pltpu.SMEM)
    exchanges = 3 * SUBITERS - 2
    return pl.pallas_call(
        functools.partial(stripe_kernel, count, scales, side),
        out_shape=jax.ShapeDtypeStruct((band, columns), jnp.float32),
        in_specs=[VMEM] * 4 + [smem] * 3 + [VMEM],
        out_specs=VMEM,
        scratch_shapes=[
            f32(*plane), f32(*plane), f32(*plane), f32(*plane),
            f32(exchanges, 2, *plane), f32(*plane), f32(2 * side + 1, *plane),
            f32(count, 2, TILE * TILE), f32(3, 8, TILE * TILE), f32(8, TILE * TILE),
            f32(3 * band, WIDTH), f32(3 * band, WIDTH), table, table, table, table,
            f32(levels, *plane), f32(SUBITERS, count, 2, LANES),
            f32(columns // LANES * 8, LANES), f32(2, 2, WIDTH, LANES),
            sem(count), sem(count), sem(SUBITERS, count), sem(SUBITERS, count), sem(2), sem(2),
            sem(exchanges, 2), sem(exchanges, 2),
            sem(SUBITERS, 2 * side + 1), sem(SUBITERS, 2 * side + 1),
        ],
        compiler_params=pltpu.CompilerParams(
            collective_id=0, has_side_effects=True, vmem_limit_bytes=56 * 1024 * 1024
        ),
    )(image_now, gradient, hessian_weight, psf, facet_of_row, tile_slot, thresholds, spline_matrices(levels))


EDGE = 80
BASE = EDGE + 8
WEIGHT_EDGE = 40
PARTS = 2
HEIGHT = PARTS * LANES


def wide(ref, start, n):
    return jnp.concatenate([ref[p, pl.ds(start, n), :] for p in range(PARTS)], axis=1)


def put(ref, start, x):
    for p in range(PARTS):
        ref[p, pl.ds(start, x.shape[0]), :] = x[:, p * LANES : (p + 1) * LANES]


def iotas(shape):
    return lax.broadcasted_iota(jnp.int32, shape, 0), lax.broadcasted_iota(jnp.int32, shape, 1)


def build_splines(splines):
    i, j = iotas((HEIGHT, HEIGHT))
    o = jnp.abs(i - j)
    for level in range(splines.shape[0]):
        d = 2**level
        coef = jnp.where(o == 0, 0.375, jnp.where(o == d, 0.25, jnp.where(o == 2 * d, 0.0625, 0.0)))
        splines[level] = coef.astype(jnp.bfloat16)


def gather_taps(pool, turned, band, taps, taps_t):
    count = pool.shape[0]
    tile = jnp.concatenate([pool[:, 0, :], pool[:, 1, :]], axis=1)
    for n in range(TILE):
        shift = TILE * (n - HALF) % (TILE * TILE)
        turned[n * count : (n + 1) * count, :] = pltpu.roll(tile, shift, 1) if shift else tile
    row, lane = iotas((HEIGHT, count))
    spread = jnp.where(row // band == lane, 1.0, 0.0).astype(jnp.bfloat16)
    row, lane = iotas((HEIGHT, LANES))
    slots = dot(spread, pool[:, 2, :].astype(jnp.bfloat16))
    slot = jnp.sum(jnp.where(lane == row % band, slots, 0.0), axis=1, keepdims=True)
    row, lane = iotas((HEIGHT, TILE * count))
    chosen = (slot == (lane % count).astype(jnp.float32)) & (row % TILE == lane // count)
    chosen = jnp.where(chosen, 1.0, 0.0).astype(jnp.bfloat16)
    for n, part in enumerate(halves(turned[...])):
        x = dot(chosen, part)
        taps[n] = x
        taps_t[n] = x.T


def build_forward(taps_t, tables):
    row, lane = iotas((HEIGHT, TILE * TILE))
    repeat = jnp.where(row % TILE == lane // TILE, 1.0, 0.0).astype(jnp.bfloat16)
    r, c = iotas((HEIGHT, HEIGHT))
    inside = (r - c + HALF >= 0) & (r - c + HALF < TILE)
    row, _ = iotas((TILE * TILE, HEIGHT))

    def one(b, carry):
        rows = pl.ds(pl.multiple_of(b * HEIGHT, HEIGHT), HEIGHT)
        for n in range(2):
            x = jnp.where(row % TILE == b, taps_t[n], 0.0).astype(jnp.bfloat16)
            tables[n, rows, :] = jnp.where(inside, dot(repeat, x), 0.0).astype(jnp.bfloat16)
        return carry

    lax.fori_loop(0, TILE, one, 0, unroll=True)


def build_adjoint(taps, tables):
    row, lane = iotas((TILE * TILE, HEIGHT))
    repeat = jnp.where(lane % TILE == row // TILE, 1.0, 0.0).astype(jnp.bfloat16)
    r, c = iotas((HEIGHT, HEIGHT))
    inside = (c - r + HALF >= 0) & (c - r + HALF < TILE)
    _, lane = iotas((HEIGHT, TILE * TILE))

    def one(b, carry):
        rows = pl.ds(pl.multiple_of(b * HEIGHT, HEIGHT), HEIGHT)
        for n in range(2):
            x = jnp.where(lane % TILE == b, taps[n], 0.0).astype(jnp.bfloat16)
            tables[n, rows, :] = jnp.where(inside, dot(x, repeat), 0.0).astype(jnp.bfloat16)
        return carry

    lax.fori_loop(0, TILE, one, 0, unroll=True)


def tile_blur(src, low, n, tables, sign, moved):
    high, rest = halves(wide(src, BASE + low - HALF, n + TILE))
    for b in range(TILE):
        rows = pl.ds(b * HEIGHT, HEIGHT)
        coarse = tables[0, rows, :]
        put(moved.at[b], 0, dot(high, coarse) + dot(rest, coarse) + dot(high, tables[1, rows, :]))
    sides = []
    for p in range(PARTS):
        total = None
        for b in range(TILE):
            x = moved[b, p, pl.ds(b if sign > 0 else TILE - b, n), :]
            total = x if total is None else total + x
        sides.append(total)
    return jnp.concatenate(sides, axis=1)


def cascade(src, levels_ref, splines, width, reaches, alive):
    for level, reach in enumerate(reaches):
        d = 2**level
        source = src if level == 0 else levels_ref.at[level - 1]
        sides = []
        for p in range(PARTS):

            def smooth(start, n):
                x = lambda o: source[p, pl.ds(BASE + start + o, n), :]
                return 0.0625 * (x(-2 * d) + x(2 * d)) + 0.25 * (x(-d) + x(d)) + 0.375 * x(0)

            own = smooth(0, width)
            if reach:
                own = jnp.concatenate(
                    [smooth(-reach, reach) * alive[0], own, smooth(width, reach) * alive[1]], axis=0
                )
            sides.append(own)
        high, low = halves(jnp.concatenate(sides, axis=1))
        put(levels_ref.at[level], BASE - reach, dot(high, splines[level]) + dot(low, splines[level]))


def thresholded(planes, moves, step, limits, p, rows):
    def level(k):
        return planes[k][p, rows, :] - step * moves[k][p, rows, :]

    smooth = level(0)
    total = None
    for k, limit in enumerate(limits):
        smoother = level(k + 1)
        detail = smooth - smoother
        part = detail - jnp.clip(detail, -limit, limit)
        total = part if total is None else total + part
        smooth = smoother
    return total + smooth


def tile_kernel(
    row_count, scales,
    image, gradient, weight, psf, facet, slot_of, thresholds,
    out,
    landed, g, x, h, new, change, pushed, descent, x_levels, d_levels, splines,
    pack, pool, turned, taps, taps_t, forward, adjoint, moved, blurred, sums, result,
    psf_send, psf_recv, move_send, move_recv, edge_send, edge_recv, sum_send, sum_recv, out_send, out_recv,
):
    count = row_count * scales
    band = image.shape[0]
    width = image.shape[1] // count
    levels = thresholds.shape[0]
    snake = row_count % 2 == 0 and scales % 2 == 0
    me = lax.axis_index("rows") * scales + lax.axis_index("scales")
    barrier = pltpu.get_barrier_semaphore()

    def device(index):
        return (index // scales, index % scales)

    def place(index):
        if not snake:
            return index
        r, s = index // scales, index % scales
        z, flat = r // 2, r % 2
        line = 2 * z + flat + (z % 2) * (1 - 2 * flat)
        y = s // 2
        y = y + (line % 2) * (scales // 2 - 1 - 2 * y)
        return (line * (scales // 2) + y) * 2 + s % 2

    def holder(position):
        if not snake:
            return position
        chip = position // 2
        line, y = chip // (scales // 2), chip % (scales // 2)
        y = y + (line % 2) * (scales // 2 - 1 - 2 * y)
        z, flat = line // 2, line % 2
        flat = flat + (z % 2) * (1 - 2 * flat)
        return (2 * z + flat) * scales + 2 * y + position % 2

    here = place(me)

    def peer(k):
        return (me + k) % count

    def columns(index):
        return pl.ds(pl.multiple_of(width * index, LANES), width)

    def stripe(index):
        return pl.ds(pl.multiple_of(band * index, band), band)

    def greet(k, carry):
        pl.semaphore_signal(barrier, inc=1, device_id=device(peer(k)), device_id_type=MESH)
        return carry

    lax.fori_loop(1, count, greet, 0)

    def copy(src, dst, send_sem, recv_sem, index):
        return pltpu.make_async_remote_copy(
            src_ref=src, dst_ref=dst, send_sem=send_sem, recv_sem=recv_sem,
            device_id=device(index), device_id_type=MESH,
        )

    def share(src, dst, send, recv, first=1, last=count):
        def start(k, carry):
            p = peer(k)
            copy(src(p), dst, send, recv, p).start()
            return carry

        lax.fori_loop(first, last, start, 0)

    def all_of(ref, send, recv):
        return copy(ref, ref, send, recv, peer(1))

    def edges(n, ref, reach):
        right = copy(ref.at[:, pl.ds(BASE + width - reach, reach)], ref.at[:, pl.ds(BASE - reach, reach)],
                     edge_send.at[n, 0], edge_recv.at[n, 0], holder((here + 1) % count))
        left = copy(ref.at[:, pl.ds(BASE, reach)], ref.at[:, pl.ds(BASE + width, reach)],
                    edge_send.at[n, 1], edge_recv.at[n, 1], holder((here + count - 1) % count))

        def start():
            @pl.when(here > 0)
            def _():
                left.start()

            @pl.when(here < count - 1)
            def _():
                right.start()

        def arrive():
            @pl.when(here > 0)
            def _():
                left.wait_send()
                right.wait_recv()

            @pl.when(here < count - 1)
            def _():
                right.wait_send()
                left.wait_recv()

        return start, arrive

    lane = lax.broadcasted_iota(jnp.int32, (1, LANES), 1)
    slots = jnp.zeros((1, LANES), jnp.float32)
    for r in range(band):
        slots = jnp.where(lane == r, slot_of[facet[r]].astype(jnp.float32), slots)
    pack[0:1, :] = psf[:, :LANES]
    pack[1:2, :] = psf[:, LANES:]
    pack[2:3, :] = slots
    pool[me] = pack[...]
    moving = [gradient, image, weight]
    for n, source in enumerate(moving):
        landed[n, stripe(me), :] = source[:, columns(here)]
    for ref in (g, x, descent):
        for p in range(PARTS):
            ref[p, pl.ds(0, BASE), :] = jnp.zeros((BASE, LANES), jnp.float32)
            ref[p, pl.ds(BASE + width, BASE), :] = jnp.zeros((BASE, LANES), jnp.float32)
    for p in range(PARTS):
        h[p, pl.ds(BASE - WEIGHT_EDGE, WEIGHT_EDGE), :] = jnp.zeros((WEIGHT_EDGE, LANES), jnp.float32)
        h[p, pl.ds(BASE + width, WEIGHT_EDGE), :] = jnp.zeros((WEIGHT_EDGE, LANES), jnp.float32)
    build_splines(splines)
    alive = [jnp.where(here > 0, 1.0, 0.0), jnp.where(here < count - 1, 1.0, 0.0)]

    pl.semaphore_wait(barrier, count - 1)
    share(lambda p: pack, pool.at[me], psf_send.at[0], psf_recv.at[0])

    def move(n, first=1, last=count):
        source = moving[n]
        share(lambda p: source.at[:, columns(place(p))], landed.at[n, stripe(me)],
              move_send.at[n], move_recv.at[n], first, last)

    move(0)
    move(1)

    others = pl.ds(0, count - 1)
    others_rows = pl.ds(0, (count - 1) * band)

    def arrived(n, ref):
        all_of(landed.at[n, others_rows], move_send.at[n], move_recv.at[n]).wait_recv()
        put(ref, BASE, landed[n].T)

    all_of(pool.at[others], psf_send.at[0], psf_recv.at[0]).wait()
    gather_taps(pool, turned, band, taps, taps_t)
    build_forward(taps_t, forward)
    arrived(0, g)
    start, g_arrive = edges(0, g, EDGE)
    start()
    move(2)
    arrived(1, x)
    start, x_arrive = edges(1, x, EDGE)
    start()
    g_arrive()
    outer = (80, 72, 64, 48)
    inner = (32, 24, 16, 0)
    blurred[...] = tile_blur(g, 0, width, forward, 1, moved)
    cascade(g, d_levels, splines, width, outer, alive)
    arrived(2, h)
    weight_start, weight_arrive = edges(2, h, WEIGHT_EDGE)

    def share_sums(sweep, moved):
        d, b, w = wide(moved, BASE, width), blurred[...], wide(h, BASE, width)

        def lanes(values):
            column = jnp.sum(values, axis=0, keepdims=True)
            return column[:, :LANES] + column[:, LANES:]

        sums[sweep, me] = jnp.concatenate([lanes(d * d), lanes(w * b * b)], axis=0)
        share(lambda p: sums.at[sweep, me], sums.at[sweep, me], sum_send.at[sweep], sum_recv.at[sweep])

    def step_of(sweep):
        all_of(sums.at[sweep, others], sum_send.at[sweep], sum_recv.at[sweep]).wait()
        totals = jnp.sum(jnp.sum(sums[sweep], axis=0), axis=1, keepdims=True)
        return totals[0:1] / totals[1:2]

    def chunks(reach):
        return [pl.ds(BASE - reach + n, 32) for n in range(0, width + 2 * reach, 32)]

    share_sums(0, g)
    weight_start()
    build_adjoint(taps, adjoint)
    x_arrive()
    cascade(x, x_levels, splines, width, outer, alive)
    step = step_of(0)
    limits = [step * thresholds[k] for k in range(levels)]
    planes = [x] + [x_levels.at[k] for k in range(levels)]
    moves = [g] + [d_levels.at[k] for k in range(levels)]
    for rows in chunks(outer[-1]):
        for p in range(PARTS):
            value = thresholded(planes, moves, step, limits, p, rows)
            new[p, rows, :] = value
            change[p, rows, :] = value - x[p, rows, :]
    weight_arrive()
    n = width + 2 * WEIGHT_EDGE
    value = tile_blur(change, -WEIGHT_EDGE, n, forward, 1, moved)
    put(pushed, BASE - WEIGHT_EDGE, value * wide(h, BASE - WEIGHT_EDGE, n))
    reach = inner[0]
    n = width + 2 * reach
    value = tile_blur(pushed, -reach, n, adjoint, -1, moved) + wide(g, BASE - reach, n)
    value = jnp.concatenate(
        [value[:reach] * alive[0], value[reach : reach + width], value[reach + width :] * alive[1]], axis=0
    )
    put(descent, BASE - reach, value)
    blurred[...] = tile_blur(descent, 0, width, forward, 1, moved)
    share_sums(1, descent)
    cascade(new, x_levels, splines, width, inner, alive)
    cascade(descent, d_levels, splines, width, inner, alive)
    step = step_of(1)
    limits = [step * thresholds[k] for k in range(levels)]
    planes[0], moves[0] = new, descent
    for rows in chunks(0):
        for p in range(PARTS):
            change[p, rows, :] = thresholded(planes, moves, step, limits, p, rows)
    result[...] = wide(change, BASE, width).T
    share(lambda p: result.at[stripe(p)], out.at[:, columns(here)], out_send.at[0], out_recv.at[0])
    out[:, columns(here)] = result[stripe(me), :]
    for n in range(len(moving)):
        all_of(landed.at[n, others_rows], move_send.at[n], move_recv.at[n]).wait_send()
    all_of(result.at[others_rows], out_send.at[0], out_recv.at[0]).wait_send()
    all_of(out.at[:, pl.ds(0, (count - 1) * width)], out_send.at[0], out_recv.at[0]).wait_recv()


def tile_body(image_now, gradient, hessian_weight, psf_tiles, facet_of_row, tile_slot, thresholds):
    band, columns = image_now.shape
    levels = thresholds.shape[0]
    rows, scales = lax.axis_size("rows"), lax.axis_size("scales")
    count = rows * scales
    width = columns // count
    f32 = lambda *shape: pltpu.VMEM(shape, jnp.float32)
    b16 = lambda *shape: pltpu.VMEM(shape, jnp.bfloat16)
    sem = lambda *shape: pltpu.SemaphoreType.DMA(shape)
    smem = pl.BlockSpec(memory_space=pltpu.SMEM)
    plane = (PARTS, width + 2 * BASE, LANES)
    table = b16(2, TILE * HEIGHT, HEIGHT)
    moved = f32(TILE, PARTS, width + 2 * EDGE, LANES)
    return pl.pallas_call(
        functools.partial(tile_kernel, rows, scales),
        out_shape=jax.ShapeDtypeStruct((band, columns), jnp.float32),
        in_specs=[VMEM] * 4 + [smem] * 3,
        out_specs=VMEM,
        scratch_shapes=[
            f32(3, HEIGHT, width), *[f32(*plane)] * 7, f32(levels, *plane), f32(levels, *plane),
            b16(levels, HEIGHT, HEIGHT),
            f32(3, LANES), f32(count, 3, LANES), f32(TILE * count, TILE * TILE),
            f32(2, HEIGHT, TILE * TILE), f32(2, TILE * TILE, HEIGHT), table, table, moved,
            f32(width, HEIGHT), f32(SUBITERS, count, 2, LANES), f32(HEIGHT, width),
            sem(1), sem(1), sem(3), sem(3), sem(3, 2), sem(3, 2), sem(SUBITERS), sem(SUBITERS), sem(1), sem(1),
        ],
        compiler_params=pltpu.CompilerParams(
            collective_id=0, has_side_effects=True, vmem_limit_bytes=56 * 1024 * 1024
        ),
    )(image_now, gradient, hessian_weight, psf_tiles, facet_of_row, tile_slot, thresholds)


def body(image_now, *rest):
    band, columns = image_now.shape
    count = lax.axis_size("rows") * lax.axis_size("scales")
    levels = rest[-1].shape[0]
    whole = columns % (count * LANES) == 0 and columns // count >= LANES and band * count == HEIGHT and levels == 4
    return (tile_body if whole else stripe_body)(image_now, *rest)


def solution(mesh):
    band = P(AXES, None)
    in_specs = (band, band, band, band, P(AXES), P(), P())
    return jax.shard_map(body, mesh=mesh, in_specs=in_specs, out_specs=band, check_vma=False)
```

```python
import functools

import jax
import jax.numpy as jnp
import numpy as np
from jax import lax
from jax.experimental import pallas as pl
from jax.experimental.pallas import tpu as pltpu
from jax.sharding import PartitionSpec as P

TILE = 16
HALF = TILE // 2
SUBITERS = 2
LANES = 128
BLOCK = 32
GROUPS = LANES // BLOCK
WIDTH = 8 * BLOCK
AXES = ("rows", "scales")
VMEM = pl.BlockSpec(memory_space=pltpu.VMEM)


def spline_matrices(levels):
    w = np.arange(WIDTH)
    same = (w[:, None] // BLOCK) == (w[None, :] // BLOCK)
    place = w % BLOCK
    nearer = place + np.where(place < BLOCK // 2, BLOCK, -BLOCK)
    planes = []
    for level in range(levels):
        d = 2**level
        for column in (place, nearer):
            o = np.abs(column[:, None] - place[None, :])
            coef = np.where(o == 0, 0.375, np.where(o == d, 0.25, np.where(o == 2 * d, 0.0625, 0.0)))
            planes.append(np.where(same, coef, 0.0))
    return jnp.asarray(np.stack(planes), jnp.bfloat16)


def halves(x):
    high = x.astype(jnp.bfloat16)
    low = (x - high.astype(jnp.float32)).astype(jnp.bfloat16)
    return high, low


def dot(a, b):
    return jnp.dot(a, b, preferred_element_type=jnp.float32)


def block_shift(x, s):
    if s == 0:
        return x
    count = x.shape[0] // GROUPS
    parts = [x[p * count : (p + 1) * count] for p in range(GROUPS)]
    row = lax.broadcasted_iota(jnp.int32, parts[0].shape, 0)
    if s == 1:
        last = jnp.where(row == count - 1, 0.0, pltpu.roll(parts[0], count - 1, 0))
        return jnp.concatenate(parts[1:] + [last], axis=0)
    first = jnp.where(row == 0, 0.0, pltpu.roll(parts[-1], 1, 0))
    return jnp.concatenate([first] + parts[:-1], axis=0)


def beside(x):
    lane = lax.broadcasted_iota(jnp.int32, x.shape, 1) % BLOCK
    return jnp.where(lane < BLOCK // 2, block_shift(x, 1), block_shift(x, -1))


def blur(stripes, high_ref, low_ref):
    total = None
    for t, x in enumerate(stripes):
        for n, y in enumerate((x, beside(x))):
            high, low = halves(y)
            w = high_ref[t * 2 + n]
            part = dot(high, w) + dot(low, w) + dot(high, low_ref[t * 2 + n])
            total = part if total is None else total + part
    return total


def to_blocks(src_ref, dst_ref, tiles):
    count = src_ref.shape[1] // LANES
    for q in range(count):
        tiles[pl.ds(8 * q, 8), :] = src_ref[:, q * LANES : (q + 1) * LANES]
    group = lax.broadcasted_iota(jnp.int32, (count, LANES), 1) // BLOCK
    for half in range(2):
        outs = [None] * GROUPS
        for k in range(4):
            a = tiles[pl.ds(half * 4 + k, count, stride=8), :]
            for p in range(GROUPS):
                shift = BLOCK * ((k - p) % 4)
                moved = pltpu.roll(a, shift, 1) if shift else a
                outs[p] = moved if k == 0 else jnp.where(group == k, moved, outs[p])
        for p in range(GROUPS):
            dst_ref[p * count : (p + 1) * count, half * LANES : (half + 1) * LANES] = outs[p]


def from_blocks(src_ref, dst_ref, tiles):
    count = dst_ref.shape[1] // LANES
    group = lax.broadcasted_iota(jnp.int32, (count, LANES), 1) // BLOCK
    for half in range(2):
        for k in range(4):
            out = None
            for p in range(GROUPS):
                x = src_ref[p * count : (p + 1) * count, half * LANES : (half + 1) * LANES]
                shift = BLOCK * ((p - k) % 4)
                moved = pltpu.roll(x, shift, 1) if shift else x
                out = moved if p == 0 else jnp.where(group == p, moved, out)
            tiles[pl.ds(half * 4 + k, count, stride=8), :] = out
    for q in range(count):
        dst_ref[:, q * LANES : (q + 1) * LANES] = tiles[pl.ds(8 * q, 8), :]


def build_weights(base_ref, lead, high_ref, low_ref, wide):
    lane = lax.broadcasted_iota(jnp.int32, (8, WIDTH), 1) % BLOCK
    for t in range(3):
        base = base_ref[8 * t : 8 * t + 8, :]
        for w in range(BLOCK):
            for n, s in enumerate((0, 1 if w < BLOCK // 2 else -1)):
                moved = pltpu.roll(base, (w - lead + BLOCK * s) % WIDTH, 1)
                x = lane - (w - lead + BLOCK * s)
                kept = jnp.where((x >= 0) & (x < TILE), moved, 0.0)
                for half in range(2):
                    wide[n, half, pl.ds(w, 8, stride=BLOCK), :] = kept[
                        :, half * LANES : (half + 1) * LANES
                    ]
        for n in range(2):
            for half in range(2):
                high, low = halves(wide[n, half])
                high_ref[t * 2 + n, :, half * LANES : (half + 1) * LANES] = high
                low_ref[t * 2 + n, :, half * LANES : (half + 1) * LANES] = low


def moved_rows(vregs, rolls, i, d):
    if d % 4 == 0:
        return vregs[i + d // 4]
    shift = (-BLOCK * d) % LANES

    def rolled(n):
        if (n, shift) not in rolls:
            rolls[(n, shift)] = pltpu.roll(vregs[n], shift, 1)
        return rolls[(n, shift)]

    lane = lax.broadcasted_iota(jnp.int32, vregs[i].shape, 1)
    if d > 0:
        return jnp.where(lane < LANES - BLOCK * d, rolled(i), rolled(i + 1))
    return jnp.where(lane >= -BLOCK * d, rolled(i), rolled(i - 1))


def column_cascade(stripe_refs, alive, levels_ref, step_rows):
    reach = len(stripe_refs) // 2
    levels = levels_ref.shape[0]

    def chunk(n, carry):
        rows = pl.ds(pl.multiple_of(n * step_rows, step_rows), step_rows)
        vregs = {}
        for t, ref in enumerate(stripe_refs):
            for half in range(2):
                vregs[2 * t + half] = ref[rows, half * LANES : (half + 1) * LANES]
        own = 2 * reach
        for level in range(levels):
            d = 2**level
            left = 2 ** (levels + 1) - 2 ** (level + 2)
            margin = -(-left // 4)
            rolls, out = {}, {}
            keys = vregs
            for i in range(own - margin, own + 2 + margin):
                outer = moved_rows(keys, rolls, i, -2 * d) + moved_rows(keys, rolls, i, 2 * d)
                inner = moved_rows(keys, rolls, i, -d) + moved_rows(keys, rolls, i, d)
                value = 0.0625 * outer + 0.25 * inner + 0.375 * keys[i]
                t = i // 2
                out[i] = value if t == reach else value * alive[t]
            vregs = out
            for half in range(2):
                levels_ref[level, rows, half * LANES : (half + 1) * LANES] = out[own + half]
        return carry

    lax.fori_loop(0, stripe_refs[0].shape[0] // step_rows, chunk, 0)


def row_cascade(levels_ref, spline_ref):
    levels = levels_ref.shape[0]
    for level in range(levels):

        def one(k, carry):
            x = levels_ref[k]
            total = None
            for n, y in enumerate((x, beside(x))):
                high, low = halves(y)
                w = spline_ref[level * 2 + n]
                part = dot(high, w) + dot(low, w)
                total = part if total is None else total + part
            levels_ref[k] = total
            return carry

        lax.fori_loop(level, levels, one, 0)


def keep(own, levels_ref, limits):
    levels = levels_ref.shape[0]
    smooth = own
    total = None
    for k in range(levels):
        smoother = levels_ref[k]
        detail = smooth - smoother
        part = detail - jnp.clip(detail, -limits[k], limits[k])
        total = part if total is None else total + part
        smooth = smoother
    return total + smooth


def build_bases(taps, flipped, forward, adjoint):
    lane = lax.broadcasted_iota(jnp.int32, (8, WIDTH), 1)
    sub = lax.broadcasted_iota(jnp.int32, (8, WIDTH), 0)
    group, inside = lane // BLOCK, lane % BLOCK < TILE
    own = flipped[...]
    turned = [pltpu.roll(own, TILE * n, 1) if n else own for n in range(TILE)]
    forward[...] = jnp.zeros_like(forward)
    for a in range(TILE):
        placed = jnp.zeros((8, WIDTH), jnp.float32)
        for r in range(8):
            placed = jnp.where((sub == r) & (group == r) & inside, turned[(2 * r - a) % TILE], placed)
        forward[a : a + 8, :] += placed
    for t in range(3):
        x = taps[t]
        row = sub + 8 * t
        tap = group - row + TILE
        placed = jnp.zeros((8, WIDTH), jnp.float32)
        for n in range(TILE):
            moved = pltpu.roll(x, TILE * n, 1) if n else x
            use = ((group + row) % TILE == n) & inside & (tap >= 0) & (tap < TILE)
            placed = jnp.where(use, moved, placed)
        adjoint[8 * t : 8 * t + 8, :] = placed


def stripe_kernel(
    count, scales, side,
    image, gradient, weight, psf, facet, slot_of, thresholds, spline,
    out,
    xi, xg, xh, current, near, middle, far, psf_all, taps, flipped, base_f, base_a, fh, fl, ah, al,
    levels, sums, tiles, wide,
    psf_send, psf_recv, sum_send, sum_recv, tap_send, tap_recv, near_send, near_recv, far_send, far_recv,
):
    me = lax.axis_index("rows") * scales + lax.axis_index("scales")
    barrier = pltpu.get_barrier_semaphore()

    def device(index):
        return (index // scales, index % scales)

    def peer(k):
        return (me + k) % count

    def exists(o):
        return (me + o >= 0) & (me + o < count)

    def greet(k, carry):
        pl.semaphore_signal(barrier, inc=1, device_id=device(peer(k)), device_id_type=MESH)
        return carry

    lax.fori_loop(1, count, greet, 0)

    def copy(src, dst, send_sem, recv_sem, index):
        return pltpu.make_async_remote_copy(
            src_ref=src, dst_ref=dst, send_sem=send_sem, recv_sem=recv_sem,
            device_id=device(index), device_id_type=MESH,
        )

    def share(src, pool, send, recv):
        def start(k, carry):
            copy(src, pool.at[me], send.at[k], recv.at[me], peer(k)).start()
            return carry

        lax.fori_loop(1, count, start, 0)

    def collect(src, pool, send, recv):
        def wait(k, carry):
            copy(src, pool.at[peer(k)], send.at[k], recv.at[peer(k)], peer(k)).wait()
            return carry

        lax.fori_loop(1, count, wait, 0)

    def spread(src, place, send, recv, offsets):
        for o in offsets:

            @pl.when(exists(o))
            def _():
                copy(src, place(-o), send(o), recv(-o), me + o).start()

    def arrive(src, place, send, recv, offsets):
        for o in offsets:

            @pl.when(exists(o))
            def _():
                copy(src, place(o), send(o), recv(o), me + o).wait()

    def near_spread(e, src):
        args = (src, lambda o: near.at[e, (o + 1) // 2], lambda o: near_send.at[e, (o + 1) // 2],
                lambda o: near_recv.at[e, (o + 1) // 2], (-1, 1))
        spread(*args)
        return lambda: arrive(*args)

    offsets = [sign * o for o in range(1, side + 1) for sign in (-1, 1)]

    evens = [0] + [o for o in offsets if o % 2 == 0]
    odds = [o for o in offsets if o % 2]
    delta = 1 - 2 * (me % 2)

    def direct(e, o):
        return copy(far.at[side], far.at[side - o], far_send.at[e, side + o], far_recv.at[e, side - o], me + o)

    def arrival(e, o):
        return copy(far.at[side], far.at[side + o], far_send.at[e, side + o], far_recv.at[e, side + o], me + o)

    def passed(e, o):
        place = o - delta + side
        return copy(far.at[side + o], far.at[place], far_send.at[e, place], far_recv.at[e, place], me + delta)

    def passes(o):
        return exists(o) & (o - delta >= -side) & (o - delta <= side)

    def far_exchange(e):
        for o in evens[1:]:

            @pl.when(exists(o))
            def _():
                direct(e, o).start()

        for o in evens:
            if o:

                @pl.when(exists(o))
                def _():
                    arrival(e, o).wait_recv()

            @pl.when(passes(o))
            def _():
                passed(e, o).start()

        for o in odds:

            @pl.when(exists(o))
            def _():
                arrival(e, o).wait_recv()

        for o in evens:
            if o:

                @pl.when(exists(o))
                def _():
                    direct(e, o).wait_send()

            @pl.when(passes(o))
            def _():
                passed(e, o).wait_send()

    to_blocks(gradient, xg, tiles)
    for o in (-1, 1):

        @pl.when(jnp.logical_not(exists(o)))
        def _():
            for e in range(near.shape[0]):
                near[e, (o + 1) // 2] = jnp.zeros(near.shape[2:], jnp.float32)
            taps[o + 1] = jnp.zeros(taps.shape[1:], jnp.float32)

    for o in offsets:

        @pl.when(jnp.logical_not(exists(o)))
        def _():
            far[o + side] = jnp.zeros(far.shape[1:], jnp.float32)

    pl.semaphore_wait(barrier, count - 1)
    share(psf, psf_all, psf_send, psf_recv)
    near_done = near_spread(0, xg)
    to_blocks(image, xi, tiles)
    to_blocks(weight, xh, tiles)
    psf_all[me] = psf[...]
    collect(psf, psf_all, psf_send, psf_recv)
    for r in range(8):
        both = psf_all[slot_of[facet[r]]]
        taps[1, r : r + 1, :] = both[0:1]
        flipped[r : r + 1, :] = both[1:2]
    tap_args = (taps.at[1], lambda o: taps.at[o + 1], lambda o: tap_send.at[(o + 1) // 2],
                lambda o: tap_recv.at[(o + 1) // 2], (-1, 1))
    spread(*tap_args)
    arrive(*tap_args)
    build_bases(taps, flipped, base_f, base_a)
    build_weights(base_f, HALF - 1, fh, fl, wide)
    alive = [None if t == side else jnp.where(exists(t - side), 1.0, 0.0) for t in range(2 * side + 1)]

    for sweep in range(SUBITERS):
        if sweep == 0:
            descent = xg
        else:
            descent = middle
            e = 3 * sweep - 2
            done = near_spread(e, current_change)
            done()
            change = current_change[...]
            pushed = xh[...] * blur([near[e, 0], change, near[e, 1]], fh, fl)
            far[side] = pushed
            near_done = near_spread(e + 1, far.at[side])
            near_done()
            middle[...] = xg[...] + blur([near[e + 1, 0], pushed, near[e + 1, 1]], ah, al)
            near_done = near_spread(e + 2, middle)
        near_done()
        e = 3 * sweep
        d = descent[...]
        b = blur([near[e, 0], d, near[e, 1]], fh, fl)

        def lanes(x):
            column = jnp.sum(x, axis=0, keepdims=True)
            return column[:, :LANES] + column[:, LANES:]

        sums[sweep, me] = jnp.concatenate([lanes(d * d), lanes(xh[...] * b * b)], axis=0)
        own = sums.at[sweep, me]
        share(own, sums.at[sweep], sum_send.at[sweep], sum_recv.at[sweep])
        if sweep == 0:
            build_weights(base_a, HALF, ah, al, wide)
        collect(own, sums.at[sweep], sum_send.at[sweep], sum_recv.at[sweep])
        totals = jnp.sum(jnp.sum(sums[sweep], axis=0), axis=1, keepdims=True)
        step = totals[0:1] / totals[1:2]
        start = xi if sweep == 0 else current
        far[side] = start[...] - step * d
        far_exchange(sweep)
        stripes = [far.at[t] for t in range(2 * side + 1)]
        column_cascade(stripes, alive, levels, 8)
        row_cascade(levels, spline)
        new = keep(far[side], levels, [step * thresholds[k] for k in range(levels.shape[0])])
        current[...] = new
        if sweep < SUBITERS - 1:
            current_change = far.at[side]
            current_change[...] = new - xi[...]
    from_blocks(current, out, tiles)


MESH = pl.DeviceIdType.MESH


def stripe_body(image_now, gradient, hessian_weight, psf_tiles, facet_of_row, tile_slot, thresholds):
    band, columns = image_now.shape
    levels = thresholds.shape[0]
    blocks = columns // BLOCK
    scales = lax.axis_size("scales")
    count = lax.axis_size("rows") * scales
    reach = 2 ** (levels + 1) - 2
    side = -(-reach // band)
    own = psf_tiles.reshape(TILE, TILE)
    psf = jnp.stack([own, jnp.flip(own, axis=1)]).reshape(2, TILE * TILE)
    plane = (blocks, WIDTH)
    table = pltpu.VMEM((6, WIDTH, WIDTH), jnp.bfloat16)
    f32 = lambda *shape: pltpu.VMEM(shape, jnp.float32)
    sem = lambda *shape: pltpu.SemaphoreType.DMA(shape)
    smem = pl.BlockSpec(memory_space=pltpu.SMEM)
    exchanges = 3 * SUBITERS - 2
    return pl.pallas_call(
        functools.partial(stripe_kernel, count, scales, side),
        out_shape=jax.ShapeDtypeStruct((band, columns), jnp.float32),
        in_specs=[VMEM] * 4 + [smem] * 3 + [VMEM],
        out_specs=VMEM,
        scratch_shapes=[
            f32(*plane), f32(*plane), f32(*plane), f32(*plane),
            f32(exchanges, 2, *plane), f32(*plane), f32(2 * side + 1, *plane),
            f32(count, 2, TILE * TILE), f32(3, 8, TILE * TILE), f32(8, TILE * TILE),
            f32(3 * band, WIDTH), f32(3 * band, WIDTH), table, table, table, table,
            f32(levels, *plane), f32(SUBITERS, count, 2, LANES),
            f32(columns // LANES * 8, LANES), f32(2, 2, WIDTH, LANES),
            sem(count), sem(count), sem(SUBITERS, count), sem(SUBITERS, count), sem(2), sem(2),
            sem(exchanges, 2), sem(exchanges, 2),
            sem(SUBITERS, 2 * side + 1), sem(SUBITERS, 2 * side + 1),
        ],
        compiler_params=pltpu.CompilerParams(
            collective_id=0, has_side_effects=True, vmem_limit_bytes=56 * 1024 * 1024
        ),
    )(image_now, gradient, hessian_weight, psf, facet_of_row, tile_slot, thresholds, spline_matrices(levels))


EDGE = 80
BASE = EDGE + 8
WEIGHT_EDGE = 40
PARTS = 2
HEIGHT = PARTS * LANES


def wide(ref, start, n):
    return jnp.concatenate([ref[p, pl.ds(start, n), :] for p in range(PARTS)], axis=1)


def put(ref, start, x):
    for p in range(PARTS):
        ref[p, pl.ds(start, x.shape[0]), :] = x[:, p * LANES : (p + 1) * LANES]


def iotas(shape):
    return lax.broadcasted_iota(jnp.int32, shape, 0), lax.broadcasted_iota(jnp.int32, shape, 1)


def build_splines(splines):
    i, j = iotas((HEIGHT, HEIGHT))
    o = jnp.abs(i - j)
    for level in range(splines.shape[0]):
        d = 2**level
        coef = jnp.where(o == 0, 0.375, jnp.where(o == d, 0.25, jnp.where(o == 2 * d, 0.0625, 0.0)))
        splines[level] = coef.astype(jnp.bfloat16)


def gather_taps(pool, turned, band, taps, taps_t):
    count = pool.shape[0]
    tile = jnp.concatenate([pool[:, 0, :], pool[:, 1, :]], axis=1)
    for n in range(TILE):
        shift = TILE * (n - HALF) % (TILE * TILE)
        turned[n * count : (n + 1) * count, :] = pltpu.roll(tile, shift, 1) if shift else tile
    row, lane = iotas((HEIGHT, count))
    spread = jnp.where(row // band == lane, 1.0, 0.0).astype(jnp.bfloat16)
    row, lane = iotas((HEIGHT, LANES))
    slots = dot(spread, pool[:, 2, :].astype(jnp.bfloat16))
    slot = jnp.sum(jnp.where(lane == row % band, slots, 0.0), axis=1, keepdims=True)
    row, lane = iotas((HEIGHT, TILE * count))
    chosen = (slot == (lane % count).astype(jnp.float32)) & (row % TILE == lane // count)
    chosen = jnp.where(chosen, 1.0, 0.0).astype(jnp.bfloat16)
    for n, part in enumerate(halves(turned[...])):
        x = dot(chosen, part)
        taps[n] = x
        taps_t[n] = x.T


def build_forward(taps_t, tables):
    row, lane = iotas((HEIGHT, TILE * TILE))
    repeat = jnp.where(row % TILE == lane // TILE, 1.0, 0.0).astype(jnp.bfloat16)
    r, c = iotas((HEIGHT, HEIGHT))
    inside = (r - c + HALF >= 0) & (r - c + HALF < TILE)
    row, _ = iotas((TILE * TILE, HEIGHT))

    def one(b, carry):
        rows = pl.ds(pl.multiple_of(b * HEIGHT, HEIGHT), HEIGHT)
        for n in range(2):
            x = jnp.where(row % TILE == b, taps_t[n], 0.0).astype(jnp.bfloat16)
            tables[n, rows, :] = jnp.where(inside, dot(repeat, x), 0.0).astype(jnp.bfloat16)
        return carry

    lax.fori_loop(0, TILE, one, 0, unroll=True)


def build_adjoint(taps, tables):
    row, lane = iotas((TILE * TILE, HEIGHT))
    repeat = jnp.where(lane % TILE == row // TILE, 1.0, 0.0).astype(jnp.bfloat16)
    r, c = iotas((HEIGHT, HEIGHT))
    inside = (c - r + HALF >= 0) & (c - r + HALF < TILE)
    _, lane = iotas((HEIGHT, TILE * TILE))

    def one(b, carry):
        rows = pl.ds(pl.multiple_of(b * HEIGHT, HEIGHT), HEIGHT)
        for n in range(2):
            x = jnp.where(lane % TILE == b, taps[n], 0.0).astype(jnp.bfloat16)
            tables[n, rows, :] = jnp.where(inside, dot(x, repeat), 0.0).astype(jnp.bfloat16)
        return carry

    lax.fori_loop(0, TILE, one, 0, unroll=True)


def tile_blur(src, low, n, tables, sign, moved):
    high, rest = halves(wide(src, BASE + low - HALF, n + TILE))
    for b in range(TILE):
        rows = pl.ds(b * HEIGHT, HEIGHT)
        coarse = tables[0, rows, :]
        put(moved.at[b], 0, dot(high, coarse) + dot(rest, coarse) + dot(high, tables[1, rows, :]))
    sides = []
    for p in range(PARTS):
        total = None
        for b in range(TILE):
            x = moved[b, p, pl.ds(b if sign > 0 else TILE - b, n), :]
            total = x if total is None else total + x
        sides.append(total)
    return jnp.concatenate(sides, axis=1)


def cascade(src, levels_ref, splines, width, reaches, alive):
    for level, reach in enumerate(reaches):
        d = 2**level
        source = src if level == 0 else levels_ref.at[level - 1]
        sides = []
        for p in range(PARTS):

            def smooth(start, n):
                x = lambda o: source[p, pl.ds(BASE + start + o, n), :]
                return 0.0625 * (x(-2 * d) + x(2 * d)) + 0.25 * (x(-d) + x(d)) + 0.375 * x(0)

            own = smooth(0, width)
            if reach:
                own = jnp.concatenate(
                    [smooth(-reach, reach) * alive[0], own, smooth(width, reach) * alive[1]], axis=0
                )
            sides.append(own)
        high, low = halves(jnp.concatenate(sides, axis=1))
        put(levels_ref.at[level], BASE - reach, dot(high, splines[level]) + dot(low, splines[level]))


def thresholded(planes, moves, step, limits, p, rows):
    def level(k):
        return planes[k][p, rows, :] - step * moves[k][p, rows, :]

    smooth = level(0)
    total = None
    for k, limit in enumerate(limits):
        smoother = level(k + 1)
        detail = smooth - smoother
        part = detail - jnp.clip(detail, -limit, limit)
        total = part if total is None else total + part
        smooth = smoother
    return total + smooth


def tile_kernel(
    row_count, scales,
    image, gradient, weight, psf, facet, slot_of, thresholds,
    out,
    landed, g, x, h, new, change, pushed, descent, x_levels, d_levels, splines,
    pack, pool, turned, taps, taps_t, forward, adjoint, moved, blurred, sums, result,
    psf_send, psf_recv, move_send, move_recv, edge_send, edge_recv, sum_send, sum_recv, out_send, out_recv,
):
    count = row_count * scales
    band = image.shape[0]
    width = image.shape[1] // count
    levels = thresholds.shape[0]
    snake = row_count % 2 == 0 and scales % 2 == 0
    me = lax.axis_index("rows") * scales + lax.axis_index("scales")
    barrier = pltpu.get_barrier_semaphore()

    def device(index):
        return (lax.div(index, scales), lax.rem(index, scales))

    def place(index):
        if not snake:
            return index
        r, s = device(index)
        z, flat = lax.div(r, 2), lax.rem(r, 2)
        line = 2 * z + flat + lax.rem(z, 2) * (1 - 2 * flat)
        y = lax.div(s, 2)
        y = y + lax.rem(line, 2) * (scales // 2 - 1 - 2 * y)
        return (line * (scales // 2) + y) * 2 + lax.rem(s, 2)

    def holder(position):
        if not snake:
            return position
        chip = lax.div(position, 2)
        line, y = lax.div(chip, scales // 2), lax.rem(chip, scales // 2)
        y = y + lax.rem(line, 2) * (scales // 2 - 1 - 2 * y)
        z, flat = lax.div(line, 2), lax.rem(line, 2)
        flat = flat + lax.rem(z, 2) * (1 - 2 * flat)
        return (2 * z + flat) * scales + 2 * y + lax.rem(position, 2)

    here = place(me)

    def peer(k):
        return lax.rem(me + k, count)

    def columns(index):
        return pl.ds(pl.multiple_of(width * index, LANES), width)

    def stripe(index):
        return pl.ds(pl.multiple_of(band * index, band), band)

    def greet(k, carry):
        pl.semaphore_signal(barrier, inc=1, device_id=device(peer(k)), device_id_type=MESH)
        return carry

    lax.fori_loop(1, count, greet, 0, unroll=True)

    def copy(src, dst, send_sem, recv_sem, index):
        return pltpu.make_async_remote_copy(
            src_ref=src, dst_ref=dst, send_sem=send_sem, recv_sem=recv_sem,
            device_id=device(index), device_id_type=MESH,
        )

    def share(src, dst, send, recv, first=1, last=count):
        def start(k, carry):
            p = peer(k)
            copy(src(p), dst, send, recv, p).start()
            return carry

        lax.fori_loop(first, last, start, 0, unroll=True)

    def all_of(ref, send, recv):
        return copy(ref, ref, send, recv, peer(1))

    def edges(n, ref, reach):
        right = copy(ref.at[:, pl.ds(BASE + width - reach, reach)], ref.at[:, pl.ds(BASE - reach, reach)],
                     edge_send.at[n, 0], edge_recv.at[n, 0], holder(lax.rem(here + 1, count)))
        left = copy(ref.at[:, pl.ds(BASE, reach)], ref.at[:, pl.ds(BASE + width, reach)],
                    edge_send.at[n, 1], edge_recv.at[n, 1], holder(lax.rem(here + count - 1, count)))

        def start():
            @pl.when(here > 0)
            def _():
                left.start()

            @pl.when(here < count - 1)
            def _():
                right.start()

        def arrive():
            @pl.when(here > 0)
            def _():
                left.wait_send()
                right.wait_recv()

            @pl.when(here < count - 1)
            def _():
                right.wait_send()
                left.wait_recv()

        return start, arrive

    lane = lax.broadcasted_iota(jnp.int32, (1, LANES), 1)
    slots = jnp.zeros((1, LANES), jnp.float32)
    for r in range(band):
        slots = jnp.where(lane == r, slot_of[facet[r]].astype(jnp.float32), slots)
    pack[0:1, :] = psf[:, :LANES]
    pack[1:2, :] = psf[:, LANES:]
    pack[2:3, :] = slots
    pool[me] = pack[...]
    moving = [gradient, image, weight]
    for n, source in enumerate(moving):
        landed[n, stripe(me), :] = source[:, columns(here)]
    for ref in (g, x, descent):
        for p in range(PARTS):
            ref[p, pl.ds(0, BASE), :] = jnp.zeros((BASE, LANES), jnp.float32)
            ref[p, pl.ds(BASE + width, BASE), :] = jnp.zeros((BASE, LANES), jnp.float32)
    for p in range(PARTS):
        h[p, pl.ds(BASE - WEIGHT_EDGE, WEIGHT_EDGE), :] = jnp.zeros((WEIGHT_EDGE, LANES), jnp.float32)
        h[p, pl.ds(BASE + width, WEIGHT_EDGE), :] = jnp.zeros((WEIGHT_EDGE, LANES), jnp.float32)
    build_splines(splines)
    alive = [jnp.where(here > 0, 1.0, 0.0), jnp.where(here < count - 1, 1.0, 0.0)]

    pl.semaphore_wait(barrier, count - 1)
    share(lambda p: pack, pool.at[me], psf_send.at[0], psf_recv.at[0])

    def move(n, first=1, last=count):
        source = moving[n]
        share(lambda p: source.at[:, columns(place(p))], landed.at[n, stripe(me)],
              move_send.at[n], move_recv.at[n], first, last)

    move(0)
    move(2, 1, count // 2)

    others = pl.ds(0, count - 1)
    others_rows = pl.ds(0, (count - 1) * band)

    def arrived(n, ref):
        all_of(landed.at[n, others_rows], move_send.at[n], move_recv.at[n]).wait_recv()
        put(ref, BASE, landed[n].T)

    all_of(pool.at[others], psf_send.at[0], psf_recv.at[0]).wait()
    gather_taps(pool, turned, band, taps, taps_t)
    build_forward(taps_t, forward)
    arrived(0, g)
    start, g_arrive = edges(0, g, EDGE)
    start()
    move(2, count // 2, count)
    move(1)
    g_arrive()
    outer = (80, 72, 64, 48)
    inner = (32, 24, 16, 0)
    blurred[...] = tile_blur(g, 0, width, forward, 1, moved)
    arrived(2, h)
    x_start, x_arrive = edges(1, x, EDGE)
    weight_start, weight_arrive = edges(2, h, WEIGHT_EDGE)

    def share_sums(sweep, moved):
        d, b, w = wide(moved, BASE, width), blurred[...], wide(h, BASE, width)

        def lanes(values):
            column = jnp.sum(values, axis=0, keepdims=True)
            return column[:, :LANES] + column[:, LANES:]

        sums[sweep, me] = jnp.concatenate([lanes(d * d), lanes(w * b * b)], axis=0)
        share(lambda p: sums.at[sweep, me], sums.at[sweep, me], sum_send.at[sweep], sum_recv.at[sweep])

    def step_of(sweep):
        all_of(sums.at[sweep, others], sum_send.at[sweep], sum_recv.at[sweep]).wait()
        totals = jnp.sum(jnp.sum(sums[sweep], axis=0), axis=1, keepdims=True)
        return totals[0:1] / totals[1:2]

    def chunks(reach):
        return [pl.ds(BASE - reach + n, 32) for n in range(0, width + 2 * reach, 32)]

    share_sums(0, g)
    cascade(g, d_levels, splines, width, outer, alive)
    arrived(1, x)
    x_start()
    weight_start()
    build_adjoint(taps, adjoint)
    x_arrive()
    cascade(x, x_levels, splines, width, outer, alive)
    step = step_of(0)
    limits = [step * thresholds[k] for k in range(levels)]
    planes = [x] + [x_levels.at[k] for k in range(levels)]
    moves = [g] + [d_levels.at[k] for k in range(levels)]
    for rows in chunks(outer[-1]):
        for p in range(PARTS):
            value = thresholded(planes, moves, step, limits, p, rows)
            new[p, rows, :] = value
            change[p, rows, :] = value - x[p, rows, :]
    weight_arrive()
    n = width + 2 * WEIGHT_EDGE
    value = tile_blur(change, -WEIGHT_EDGE, n, forward, 1, moved)
    put(pushed, BASE - WEIGHT_EDGE, value * wide(h, BASE - WEIGHT_EDGE, n))
    reach = inner[0]
    n = width + 2 * reach
    value = tile_blur(pushed, -reach, n, adjoint, -1, moved) + wide(g, BASE - reach, n)
    value = jnp.concatenate(
        [value[:reach] * alive[0], value[reach : reach + width], value[reach + width :] * alive[1]], axis=0
    )
    put(descent, BASE - reach, value)
    blurred[...] = tile_blur(descent, 0, width, forward, 1, moved)
    share_sums(1, descent)
    cascade(new, x_levels, splines, width, inner, alive)
    cascade(descent, d_levels, splines, width, inner, alive)
    step = step_of(1)
    limits = [step * thresholds[k] for k in range(levels)]
    planes[0], moves[0] = new, descent
    for rows in chunks(0):
        for p in range(PARTS):
            change[p, rows, :] = thresholded(planes, moves, step, limits, p, rows)
    result[...] = wide(change, BASE, width).T
    share(lambda p: result.at[stripe(p)], out.at[:, columns(here)], out_send.at[0], out_recv.at[0])
    out[:, columns(here)] = result[stripe(me), :]
    for n in range(len(moving)):
        all_of(landed.at[n, others_rows], move_send.at[n], move_recv.at[n]).wait_send()
    all_of(result.at[others_rows], out_send.at[0], out_recv.at[0]).wait_send()
    all_of(out.at[:, pl.ds(0, (count - 1) * width)], out_send.at[0], out_recv.at[0]).wait_recv()


def tile_body(image_now, gradient, hessian_weight, psf_tiles, facet_of_row, tile_slot, thresholds):
    band, columns = image_now.shape
    levels = thresholds.shape[0]
    rows, scales = lax.axis_size("rows"), lax.axis_size("scales")
    count = rows * scales
    width = columns // count
    f32 = lambda *shape: pltpu.VMEM(shape, jnp.float32)
    b16 = lambda *shape: pltpu.VMEM(shape, jnp.bfloat16)
    sem = lambda *shape: pltpu.SemaphoreType.DMA(shape)
    smem = pl.BlockSpec(memory_space=pltpu.SMEM)
    plane = (PARTS, width + 2 * BASE, LANES)
    table = b16(2, TILE * HEIGHT, HEIGHT)
    moved = f32(TILE, PARTS, width + 2 * EDGE, LANES)
    return pl.pallas_call(
        functools.partial(tile_kernel, rows, scales),
        out_shape=jax.ShapeDtypeStruct((band, columns), jnp.float32),
        in_specs=[VMEM] * 4 + [smem] * 3,
        out_specs=VMEM,
        scratch_shapes=[
            f32(3, HEIGHT, width), *[f32(*plane)] * 7, f32(levels, *plane), f32(levels, *plane),
            b16(levels, HEIGHT, HEIGHT),
            f32(3, LANES), f32(count, 3, LANES), f32(TILE * count, TILE * TILE),
            f32(2, HEIGHT, TILE * TILE), f32(2, TILE * TILE, HEIGHT), table, table, moved,
            f32(width, HEIGHT), f32(SUBITERS, count, 2, LANES), f32(HEIGHT, width),
            sem(1), sem(1), sem(3), sem(3), sem(3, 2), sem(3, 2), sem(SUBITERS), sem(SUBITERS), sem(1), sem(1),
        ],
        compiler_params=pltpu.CompilerParams(
            collective_id=0, has_side_effects=True, vmem_limit_bytes=56 * 1024 * 1024
        ),
    )(image_now, gradient, hessian_weight, psf_tiles, facet_of_row, tile_slot, thresholds)


def body(image_now, *rest):
    band, columns = image_now.shape
    count = lax.axis_size("rows") * lax.axis_size("scales")
    levels = rest[-1].shape[0]
    whole = columns % (count * LANES) == 0 and columns // count >= LANES and band * count == HEIGHT and levels == 4
    return (tile_body if whole else stripe_body)(image_now, *rest)


def solution(mesh):
    band = P(AXES, None)
    in_specs = (band, band, band, band, P(AXES), P(), P())
    return jax.shard_map(body, mesh=mesh, in_specs=in_specs, out_specs=band, check_vma=False)
```

```python
import functools

import jax
import jax.numpy as jnp
import numpy as np
from jax import lax
from jax.experimental import pallas as pl
from jax.experimental.pallas import tpu as pltpu
from jax.sharding import PartitionSpec as P

TILE = 16
HALF = TILE // 2
SUBITERS = 2
LANES = 128
BLOCK = 32
GROUPS = LANES // BLOCK
WIDTH = 8 * BLOCK
AXES = ("rows", "scales")
VMEM = pl.BlockSpec(memory_space=pltpu.VMEM)


def spline_matrices(levels):
    w = np.arange(WIDTH)
    same = (w[:, None] // BLOCK) == (w[None, :] // BLOCK)
    place = w % BLOCK
    nearer = place + np.where(place < BLOCK // 2, BLOCK, -BLOCK)
    planes = []
    for level in range(levels):
        d = 2**level
        for column in (place, nearer):
            o = np.abs(column[:, None] - place[None, :])
            coef = np.where(o == 0, 0.375, np.where(o == d, 0.25, np.where(o == 2 * d, 0.0625, 0.0)))
            planes.append(np.where(same, coef, 0.0))
    return jnp.asarray(np.stack(planes), jnp.bfloat16)


def halves(x):
    high = x.astype(jnp.bfloat16)
    low = (x - high.astype(jnp.float32)).astype(jnp.bfloat16)
    return high, low


def dot(a, b):
    return jnp.dot(a, b, preferred_element_type=jnp.float32)


def block_shift(x, s):
    if s == 0:
        return x
    count = x.shape[0] // GROUPS
    parts = [x[p * count : (p + 1) * count] for p in range(GROUPS)]
    row = lax.broadcasted_iota(jnp.int32, parts[0].shape, 0)
    if s == 1:
        last = jnp.where(row == count - 1, 0.0, pltpu.roll(parts[0], count - 1, 0))
        return jnp.concatenate(parts[1:] + [last], axis=0)
    first = jnp.where(row == 0, 0.0, pltpu.roll(parts[-1], 1, 0))
    return jnp.concatenate([first] + parts[:-1], axis=0)


def beside(x):
    lane = lax.broadcasted_iota(jnp.int32, x.shape, 1) % BLOCK
    return jnp.where(lane < BLOCK // 2, block_shift(x, 1), block_shift(x, -1))


def blur(stripes, high_ref, low_ref):
    total = None
    for t, x in enumerate(stripes):
        for n, y in enumerate((x, beside(x))):
            high, low = halves(y)
            w = high_ref[t * 2 + n]
            part = dot(high, w) + dot(low, w) + dot(high, low_ref[t * 2 + n])
            total = part if total is None else total + part
    return total


def to_blocks(src_ref, dst_ref, tiles):
    count = src_ref.shape[1] // LANES
    for q in range(count):
        tiles[pl.ds(8 * q, 8), :] = src_ref[:, q * LANES : (q + 1) * LANES]
    group = lax.broadcasted_iota(jnp.int32, (count, LANES), 1) // BLOCK
    for half in range(2):
        outs = [None] * GROUPS
        for k in range(4):
            a = tiles[pl.ds(half * 4 + k, count, stride=8), :]
            for p in range(GROUPS):
                shift = BLOCK * ((k - p) % 4)
                moved = pltpu.roll(a, shift, 1) if shift else a
                outs[p] = moved if k == 0 else jnp.where(group == k, moved, outs[p])
        for p in range(GROUPS):
            dst_ref[p * count : (p + 1) * count, half * LANES : (half + 1) * LANES] = outs[p]


def from_blocks(src_ref, dst_ref, tiles):
    count = dst_ref.shape[1] // LANES
    group = lax.broadcasted_iota(jnp.int32, (count, LANES), 1) // BLOCK
    for half in range(2):
        for k in range(4):
            out = None
            for p in range(GROUPS):
                x = src_ref[p * count : (p + 1) * count, half * LANES : (half + 1) * LANES]
                shift = BLOCK * ((p - k) % 4)
                moved = pltpu.roll(x, shift, 1) if shift else x
                out = moved if p == 0 else jnp.where(group == p, moved, out)
            tiles[pl.ds(half * 4 + k, count, stride=8), :] = out
    for q in range(count):
        dst_ref[:, q * LANES : (q + 1) * LANES] = tiles[pl.ds(8 * q, 8), :]


def build_weights(base_ref, lead, high_ref, low_ref, wide):
    lane = lax.broadcasted_iota(jnp.int32, (8, WIDTH), 1) % BLOCK
    for t in range(3):
        base = base_ref[8 * t : 8 * t + 8, :]
        for w in range(BLOCK):
            for n, s in enumerate((0, 1 if w < BLOCK // 2 else -1)):
                moved = pltpu.roll(base, (w - lead + BLOCK * s) % WIDTH, 1)
                x = lane - (w - lead + BLOCK * s)
                kept = jnp.where((x >= 0) & (x < TILE), moved, 0.0)
                for half in range(2):
                    wide[n, half, pl.ds(w, 8, stride=BLOCK), :] = kept[
                        :, half * LANES : (half + 1) * LANES
                    ]
        for n in range(2):
            for half in range(2):
                high, low = halves(wide[n, half])
                high_ref[t * 2 + n, :, half * LANES : (half + 1) * LANES] = high
                low_ref[t * 2 + n, :, half * LANES : (half + 1) * LANES] = low


def moved_rows(vregs, rolls, i, d):
    if d % 4 == 0:
        return vregs[i + d // 4]
    shift = (-BLOCK * d) % LANES

    def rolled(n):
        if (n, shift) not in rolls:
            rolls[(n, shift)] = pltpu.roll(vregs[n], shift, 1)
        return rolls[(n, shift)]

    lane = lax.broadcasted_iota(jnp.int32, vregs[i].shape, 1)
    if d > 0:
        return jnp.where(lane < LANES - BLOCK * d, rolled(i), rolled(i + 1))
    return jnp.where(lane >= -BLOCK * d, rolled(i), rolled(i - 1))


def column_cascade(stripe_refs, alive, levels_ref, step_rows):
    reach = len(stripe_refs) // 2
    levels = levels_ref.shape[0]

    def chunk(n, carry):
        rows = pl.ds(pl.multiple_of(n * step_rows, step_rows), step_rows)
        vregs = {}
        for t, ref in enumerate(stripe_refs):
            for half in range(2):
                vregs[2 * t + half] = ref[rows, half * LANES : (half + 1) * LANES]
        own = 2 * reach
        for level in range(levels):
            d = 2**level
            left = 2 ** (levels + 1) - 2 ** (level + 2)
            margin = -(-left // 4)
            rolls, out = {}, {}
            keys = vregs
            for i in range(own - margin, own + 2 + margin):
                outer = moved_rows(keys, rolls, i, -2 * d) + moved_rows(keys, rolls, i, 2 * d)
                inner = moved_rows(keys, rolls, i, -d) + moved_rows(keys, rolls, i, d)
                value = 0.0625 * outer + 0.25 * inner + 0.375 * keys[i]
                t = i // 2
                out[i] = value if t == reach else value * alive[t]
            vregs = out
            for half in range(2):
                levels_ref[level, rows, half * LANES : (half + 1) * LANES] = out[own + half]
        return carry

    lax.fori_loop(0, stripe_refs[0].shape[0] // step_rows, chunk, 0)


def row_cascade(levels_ref, spline_ref):
    levels = levels_ref.shape[0]
    for level in range(levels):

        def one(k, carry):
            x = levels_ref[k]
            total = None
            for n, y in enumerate((x, beside(x))):
                high, low = halves(y)
                w = spline_ref[level * 2 + n]
                part = dot(high, w) + dot(low, w)
                total = part if total is None else total + part
            levels_ref[k] = total
            return carry

        lax.fori_loop(level, levels, one, 0)


def keep(own, levels_ref, limits):
    levels = levels_ref.shape[0]
    smooth = own
    total = None
    for k in range(levels):
        smoother = levels_ref[k]
        detail = smooth - smoother
        part = detail - jnp.clip(detail, -limits[k], limits[k])
        total = part if total is None else total + part
        smooth = smoother
    return total + smooth


def build_bases(taps, flipped, forward, adjoint):
    lane = lax.broadcasted_iota(jnp.int32, (8, WIDTH), 1)
    sub = lax.broadcasted_iota(jnp.int32, (8, WIDTH), 0)
    group, inside = lane // BLOCK, lane % BLOCK < TILE
    own = flipped[...]
    turned = [pltpu.roll(own, TILE * n, 1) if n else own for n in range(TILE)]
    forward[...] = jnp.zeros_like(forward)
    for a in range(TILE):
        placed = jnp.zeros((8, WIDTH), jnp.float32)
        for r in range(8):
            placed = jnp.where((sub == r) & (group == r) & inside, turned[(2 * r - a) % TILE], placed)
        forward[a : a + 8, :] += placed
    for t in range(3):
        x = taps[t]
        row = sub + 8 * t
        tap = group - row + TILE
        placed = jnp.zeros((8, WIDTH), jnp.float32)
        for n in range(TILE):
            moved = pltpu.roll(x, TILE * n, 1) if n else x
            use = ((group + row) % TILE == n) & inside & (tap >= 0) & (tap < TILE)
            placed = jnp.where(use, moved, placed)
        adjoint[8 * t : 8 * t + 8, :] = placed


def stripe_kernel(
    count, scales, side,
    image, gradient, weight, psf, facet, slot_of, thresholds, spline,
    out,
    xi, xg, xh, current, near, middle, far, psf_all, taps, flipped, base_f, base_a, fh, fl, ah, al,
    levels, sums, tiles, wide,
    psf_send, psf_recv, sum_send, sum_recv, tap_send, tap_recv, near_send, near_recv, far_send, far_recv,
):
    me = lax.axis_index("rows") * scales + lax.axis_index("scales")
    barrier = pltpu.get_barrier_semaphore()

    def device(index):
        return (index // scales, index % scales)

    def peer(k):
        return (me + k) % count

    def exists(o):
        return (me + o >= 0) & (me + o < count)

    def greet(k, carry):
        pl.semaphore_signal(barrier, inc=1, device_id=device(peer(k)), device_id_type=MESH)
        return carry

    lax.fori_loop(1, count, greet, 0)

    def copy(src, dst, send_sem, recv_sem, index):
        return pltpu.make_async_remote_copy(
            src_ref=src, dst_ref=dst, send_sem=send_sem, recv_sem=recv_sem,
            device_id=device(index), device_id_type=MESH,
        )

    def share(src, pool, send, recv):
        def start(k, carry):
            copy(src, pool.at[me], send.at[k], recv.at[me], peer(k)).start()
            return carry

        lax.fori_loop(1, count, start, 0)

    def collect(src, pool, send, recv):
        def wait(k, carry):
            copy(src, pool.at[peer(k)], send.at[k], recv.at[peer(k)], peer(k)).wait()
            return carry

        lax.fori_loop(1, count, wait, 0)

    def spread(src, place, send, recv, offsets):
        for o in offsets:

            @pl.when(exists(o))
            def _():
                copy(src, place(-o), send(o), recv(-o), me + o).start()

    def arrive(src, place, send, recv, offsets):
        for o in offsets:

            @pl.when(exists(o))
            def _():
                copy(src, place(o), send(o), recv(o), me + o).wait()

    def near_spread(e, src):
        args = (src, lambda o: near.at[e, (o + 1) // 2], lambda o: near_send.at[e, (o + 1) // 2],
                lambda o: near_recv.at[e, (o + 1) // 2], (-1, 1))
        spread(*args)
        return lambda: arrive(*args)

    offsets = [sign * o for o in range(1, side + 1) for sign in (-1, 1)]

    evens = [0] + [o for o in offsets if o % 2 == 0]
    odds = [o for o in offsets if o % 2]
    delta = 1 - 2 * (me % 2)

    def direct(e, o):
        return copy(far.at[side], far.at[side - o], far_send.at[e, side + o], far_recv.at[e, side - o], me + o)

    def arrival(e, o):
        return copy(far.at[side], far.at[side + o], far_send.at[e, side + o], far_recv.at[e, side + o], me + o)

    def passed(e, o):
        place = o - delta + side
        return copy(far.at[side + o], far.at[place], far_send.at[e, place], far_recv.at[e, place], me + delta)

    def passes(o):
        return exists(o) & (o - delta >= -side) & (o - delta <= side)

    def far_exchange(e):
        for o in evens[1:]:

            @pl.when(exists(o))
            def _():
                direct(e, o).start()

        for o in evens:
            if o:

                @pl.when(exists(o))
                def _():
                    arrival(e, o).wait_recv()

            @pl.when(passes(o))
            def _():
                passed(e, o).start()

        for o in odds:

            @pl.when(exists(o))
            def _():
                arrival(e, o).wait_recv()

        for o in evens:
            if o:

                @pl.when(exists(o))
                def _():
                    direct(e, o).wait_send()

            @pl.when(passes(o))
            def _():
                passed(e, o).wait_send()

    to_blocks(gradient, xg, tiles)
    for o in (-1, 1):

        @pl.when(jnp.logical_not(exists(o)))
        def _():
            for e in range(near.shape[0]):
                near[e, (o + 1) // 2] = jnp.zeros(near.shape[2:], jnp.float32)
            taps[o + 1] = jnp.zeros(taps.shape[1:], jnp.float32)

    for o in offsets:

        @pl.when(jnp.logical_not(exists(o)))
        def _():
            far[o + side] = jnp.zeros(far.shape[1:], jnp.float32)

    pl.semaphore_wait(barrier, count - 1)
    share(psf, psf_all, psf_send, psf_recv)
    near_done = near_spread(0, xg)
    to_blocks(image, xi, tiles)
    to_blocks(weight, xh, tiles)
    psf_all[me] = psf[...]
    collect(psf, psf_all, psf_send, psf_recv)
    for r in range(8):
        both = psf_all[slot_of[facet[r]]]
        taps[1, r : r + 1, :] = both[0:1]
        flipped[r : r + 1, :] = both[1:2]
    tap_args = (taps.at[1], lambda o: taps.at[o + 1], lambda o: tap_send.at[(o + 1) // 2],
                lambda o: tap_recv.at[(o + 1) // 2], (-1, 1))
    spread(*tap_args)
    arrive(*tap_args)
    build_bases(taps, flipped, base_f, base_a)
    build_weights(base_f, HALF - 1, fh, fl, wide)
    alive = [None if t == side else jnp.where(exists(t - side), 1.0, 0.0) for t in range(2 * side + 1)]

    for sweep in range(SUBITERS):
        if sweep == 0:
            descent = xg
        else:
            descent = middle
            e = 3 * sweep - 2
            done = near_spread(e, current_change)
            done()
            change = current_change[...]
            pushed = xh[...] * blur([near[e, 0], change, near[e, 1]], fh, fl)
            far[side] = pushed
            near_done = near_spread(e + 1, far.at[side])
            near_done()
            middle[...] = xg[...] + blur([near[e + 1, 0], pushed, near[e + 1, 1]], ah, al)
            near_done = near_spread(e + 2, middle)
        near_done()
        e = 3 * sweep
        d = descent[...]
        b = blur([near[e, 0], d, near[e, 1]], fh, fl)

        def lanes(x):
            column = jnp.sum(x, axis=0, keepdims=True)
            return column[:, :LANES] + column[:, LANES:]

        sums[sweep, me] = jnp.concatenate([lanes(d * d), lanes(xh[...] * b * b)], axis=0)
        own = sums.at[sweep, me]
        share(own, sums.at[sweep], sum_send.at[sweep], sum_recv.at[sweep])
        if sweep == 0:
            build_weights(base_a, HALF, ah, al, wide)
        collect(own, sums.at[sweep], sum_send.at[sweep], sum_recv.at[sweep])
        totals = jnp.sum(jnp.sum(sums[sweep], axis=0), axis=1, keepdims=True)
        step = totals[0:1] / totals[1:2]
        start = xi if sweep == 0 else current
        far[side] = start[...] - step * d
        far_exchange(sweep)
        stripes = [far.at[t] for t in range(2 * side + 1)]
        column_cascade(stripes, alive, levels, 8)
        row_cascade(levels, spline)
        new = keep(far[side], levels, [step * thresholds[k] for k in range(levels.shape[0])])
        current[...] = new
        if sweep < SUBITERS - 1:
            current_change = far.at[side]
            current_change[...] = new - xi[...]
    from_blocks(current, out, tiles)


MESH = pl.DeviceIdType.MESH


def stripe_body(image_now, gradient, hessian_weight, psf_tiles, facet_of_row, tile_slot, thresholds):
    band, columns = image_now.shape
    levels = thresholds.shape[0]
    blocks = columns // BLOCK
    scales = lax.axis_size("scales")
    count = lax.axis_size("rows") * scales
    reach = 2 ** (levels + 1) - 2
    side = -(-reach // band)
    own = psf_tiles.reshape(TILE, TILE)
    psf = jnp.stack([own, jnp.flip(own, axis=1)]).reshape(2, TILE * TILE)
    plane = (blocks, WIDTH)
    table = pltpu.VMEM((6, WIDTH, WIDTH), jnp.bfloat16)
    f32 = lambda *shape: pltpu.VMEM(shape, jnp.float32)
    sem = lambda *shape: pltpu.SemaphoreType.DMA(shape)
    smem = pl.BlockSpec(memory_space=pltpu.SMEM)
    exchanges = 3 * SUBITERS - 2
    return pl.pallas_call(
        functools.partial(stripe_kernel, count, scales, side),
        out_shape=jax.ShapeDtypeStruct((band, columns), jnp.float32),
        in_specs=[VMEM] * 4 + [smem] * 3 + [VMEM],
        out_specs=VMEM,
        scratch_shapes=[
            f32(*plane), f32(*plane), f32(*plane), f32(*plane),
            f32(exchanges, 2, *plane), f32(*plane), f32(2 * side + 1, *plane),
            f32(count, 2, TILE * TILE), f32(3, 8, TILE * TILE), f32(8, TILE * TILE),
            f32(3 * band, WIDTH), f32(3 * band, WIDTH), table, table, table, table,
            f32(levels, *plane), f32(SUBITERS, count, 2, LANES),
            f32(columns // LANES * 8, LANES), f32(2, 2, WIDTH, LANES),
            sem(count), sem(count), sem(SUBITERS, count), sem(SUBITERS, count), sem(2), sem(2),
            sem(exchanges, 2), sem(exchanges, 2),
            sem(SUBITERS, 2 * side + 1), sem(SUBITERS, 2 * side + 1),
        ],
        compiler_params=pltpu.CompilerParams(
            collective_id=0, has_side_effects=True, vmem_limit_bytes=56 * 1024 * 1024
        ),
    )(image_now, gradient, hessian_weight, psf, facet_of_row, tile_slot, thresholds, spline_matrices(levels))


EDGE = 80
BASE = EDGE + 8
WEIGHT_EDGE = 40
PARTS = 2
HEIGHT = PARTS * LANES


def wide(ref, start, n):
    return jnp.concatenate([ref[p, pl.ds(start, n), :] for p in range(PARTS)], axis=1)


def put(ref, start, x):
    for p in range(PARTS):
        ref[p, pl.ds(start, x.shape[0]), :] = x[:, p * LANES : (p + 1) * LANES]


def iotas(shape):
    return lax.broadcasted_iota(jnp.int32, shape, 0), lax.broadcasted_iota(jnp.int32, shape, 1)


def build_splines(splines):
    i, j = iotas((HEIGHT, HEIGHT))
    o = jnp.abs(i - j)
    for level in range(splines.shape[0]):
        d = 2**level
        coef = jnp.where(o == 0, 0.375, jnp.where(o == d, 0.25, jnp.where(o == 2 * d, 0.0625, 0.0)))
        splines[level] = coef.astype(jnp.bfloat16)


def gather_taps(pool, turned, band, taps, taps_t):
    count = pool.shape[0]
    tile = jnp.concatenate([pool[:, 0, :], pool[:, 1, :]], axis=1)
    for n in range(TILE):
        shift = TILE * (n - HALF) % (TILE * TILE)
        turned[n * count : (n + 1) * count, :] = pltpu.roll(tile, shift, 1) if shift else tile
    row, lane = iotas((HEIGHT, count))
    spread = jnp.where(row // band == lane, 1.0, 0.0).astype(jnp.bfloat16)
    row, lane = iotas((HEIGHT, LANES))
    slots = dot(spread, pool[:, 2, :].astype(jnp.bfloat16))
    slot = jnp.sum(jnp.where(lane == row % band, slots, 0.0), axis=1, keepdims=True)
    row, lane = iotas((HEIGHT, TILE * count))
    chosen = (slot == (lane % count).astype(jnp.float32)) & (row % TILE == lane // count)
    chosen = jnp.where(chosen, 1.0, 0.0).astype(jnp.bfloat16)
    for n, part in enumerate(halves(turned[...])):
        x = dot(chosen, part)
        taps[n] = x
        taps_t[n] = x.T


def build_forward(taps_t, tables):
    row, lane = iotas((HEIGHT, TILE * TILE))
    repeat = jnp.where(row % TILE == lane // TILE, 1.0, 0.0).astype(jnp.bfloat16)
    r, c = iotas((HEIGHT, HEIGHT))
    inside = (r - c + HALF >= 0) & (r - c + HALF < TILE)
    row, _ = iotas((TILE * TILE, HEIGHT))

    def one(b, carry):
        rows = pl.ds(pl.multiple_of(b * HEIGHT, HEIGHT), HEIGHT)
        for n in range(2):
            x = jnp.where(row % TILE == b, taps_t[n], 0.0).astype(jnp.bfloat16)
            tables[n, rows, :] = jnp.where(inside, dot(repeat, x), 0.0).astype(jnp.bfloat16)
        return carry

    lax.fori_loop(0, TILE, one, 0, unroll=True)


def build_adjoint(taps, tables):
    row, lane = iotas((TILE * TILE, HEIGHT))
    repeat = jnp.where(lane % TILE == row // TILE, 1.0, 0.0).astype(jnp.bfloat16)
    r, c = iotas((HEIGHT, HEIGHT))
    inside = (c - r + HALF >= 0) & (c - r + HALF < TILE)
    _, lane = iotas((HEIGHT, TILE * TILE))

    def one(b, carry):
        rows = pl.ds(pl.multiple_of(b * HEIGHT, HEIGHT), HEIGHT)
        for n in range(2):
            x = jnp.where(lane % TILE == b, taps[n], 0.0).astype(jnp.bfloat16)
            tables[n, rows, :] = jnp.where(inside, dot(x, repeat), 0.0).astype(jnp.bfloat16)
        return carry

    lax.fori_loop(0, TILE, one, 0, unroll=True)


def tile_blur(src, low, n, tables, sign, moved):
    high, rest = halves(wide(src, BASE + low - HALF, n + TILE))
    for b in range(TILE):
        rows = pl.ds(b * HEIGHT, HEIGHT)
        coarse = tables[0, rows, :]
        put(moved.at[b], 0, dot(high, coarse) + dot(rest, coarse) + dot(high, tables[1, rows, :]))
    sides = []
    for p in range(PARTS):
        total = None
        for b in range(TILE):
            x = moved[b, p, pl.ds(b if sign > 0 else TILE - b, n), :]
            total = x if total is None else total + x
        sides.append(total)
    return jnp.concatenate(sides, axis=1)


def cascade(src, levels_ref, splines, width, reaches, alive):
    for level, reach in enumerate(reaches):
        d = 2**level
        source = src if level == 0 else levels_ref.at[level - 1]
        sides = []
        for p in range(PARTS):

            def smooth(start, n):
                x = lambda o: source[p, pl.ds(BASE + start + o, n), :]
                return 0.0625 * (x(-2 * d) + x(2 * d)) + 0.25 * (x(-d) + x(d)) + 0.375 * x(0)

            own = smooth(0, width)
            if reach:
                own = jnp.concatenate(
                    [smooth(-reach, reach) * alive[0], own, smooth(width, reach) * alive[1]], axis=0
                )
            sides.append(own)
        high, low = halves(jnp.concatenate(sides, axis=1))
        put(levels_ref.at[level], BASE - reach, dot(high, splines[level]) + dot(low, splines[level]))


def thresholded(planes, moves, step, limits, p, rows):
    def level(k):
        return planes[k][p, rows, :] - step * moves[k][p, rows, :]

    smooth = level(0)
    total = None
    for k, limit in enumerate(limits):
        smoother = level(k + 1)
        detail = smooth - smoother
        part = detail - jnp.clip(detail, -limit, limit)
        total = part if total is None else total + part
        smooth = smoother
    return total + smooth


def tile_kernel(
    row_count, scales,
    image, gradient, weight, psf, facet, slot_of, thresholds,
    out,
    landed, g, x, h, new, change, pushed, descent, x_levels, d_levels, splines,
    pack, pool, turned, taps, taps_t, forward, adjoint, moved, blurred, sums, result,
    psf_send, psf_recv, move_send, move_recv, edge_send, edge_recv, sum_send, sum_recv, out_send, out_recv, keep_sem,
):
    count = row_count * scales
    band = image.shape[0]
    width = image.shape[1] // count
    levels = thresholds.shape[0]
    snake = row_count % 2 == 0 and scales % 2 == 0
    me = lax.axis_index("rows") * scales + lax.axis_index("scales")
    barrier = pltpu.get_barrier_semaphore()

    def device(index):
        return (lax.div(index, scales), lax.rem(index, scales))

    def place(index):
        if not snake:
            return index
        r, s = device(index)
        z, flat = lax.div(r, 2), lax.rem(r, 2)
        line = 2 * z + flat + lax.rem(z, 2) * (1 - 2 * flat)
        y = lax.div(s, 2)
        y = y + lax.rem(line, 2) * (scales // 2 - 1 - 2 * y)
        return (line * (scales // 2) + y) * 2 + lax.rem(s, 2)

    def holder(position):
        if not snake:
            return position
        chip = lax.div(position, 2)
        line, y = lax.div(chip, scales // 2), lax.rem(chip, scales // 2)
        y = y + lax.rem(line, 2) * (scales // 2 - 1 - 2 * y)
        z, flat = lax.div(line, 2), lax.rem(line, 2)
        flat = flat + lax.rem(z, 2) * (1 - 2 * flat)
        return (2 * z + flat) * scales + 2 * y + lax.rem(position, 2)

    here = place(me)

    def peer(k):
        return lax.rem(me + k, count)

    def columns(index):
        return pl.ds(pl.multiple_of(width * index, LANES), width)

    def stripe(index):
        return pl.ds(pl.multiple_of(band * index, band), band)

    def greet(k, carry):
        pl.semaphore_signal(barrier, inc=1, device_id=device(peer(k)), device_id_type=MESH)
        return carry

    lax.fori_loop(1, count, greet, 0, unroll=True)

    def copy(src, dst, send_sem, recv_sem, index):
        return pltpu.make_async_remote_copy(
            src_ref=src, dst_ref=dst, send_sem=send_sem, recv_sem=recv_sem,
            device_id=device(index), device_id_type=MESH,
        )

    def share(src, dst, send, recv, first=1, last=count):
        def start(k, carry):
            p = peer(k)
            copy(src(p), dst, send, recv, p).start()
            return carry

        lax.fori_loop(first, last, start, 0, unroll=True)

    def all_of(ref, send, recv):
        return copy(ref, ref, send, recv, peer(1))

    def edges(n, ref, reach):
        right = copy(ref.at[:, pl.ds(BASE + width - reach, reach)], ref.at[:, pl.ds(BASE - reach, reach)],
                     edge_send.at[n, 0], edge_recv.at[n, 0], holder(lax.rem(here + 1, count)))
        left = copy(ref.at[:, pl.ds(BASE, reach)], ref.at[:, pl.ds(BASE + width, reach)],
                    edge_send.at[n, 1], edge_recv.at[n, 1], holder(lax.rem(here + count - 1, count)))

        def start():
            @pl.when(here > 0)
            def _():
                left.start()

            @pl.when(here < count - 1)
            def _():
                right.start()

        def arrive():
            @pl.when(here > 0)
            def _():
                left.wait_send()
                right.wait_recv()

            @pl.when(here < count - 1)
            def _():
                right.wait_send()
                left.wait_recv()

        return start, arrive

    lane = lax.broadcasted_iota(jnp.int32, (1, LANES), 1)
    slots = jnp.zeros((1, LANES), jnp.float32)
    for r in range(band):
        slots = jnp.where(lane == r, slot_of[facet[r]].astype(jnp.float32), slots)
    pack[0:1, :] = psf[:, :LANES]
    pack[1:2, :] = psf[:, LANES:]
    pack[2:3, :] = slots
    pool[me] = pack[...]
    moving = [gradient, image, weight]
    kept = [
        pltpu.make_async_copy(source.at[:, columns(here)], landed.at[n, stripe(me)], keep_sem.at[n])
        for n, source in enumerate(moving)
    ]
    for c in kept:
        c.start()
    for ref in (g, x, descent):
        for p in range(PARTS):
            ref[p, pl.ds(0, BASE), :] = jnp.zeros((BASE, LANES), jnp.float32)
            ref[p, pl.ds(BASE + width, BASE), :] = jnp.zeros((BASE, LANES), jnp.float32)
    for p in range(PARTS):
        h[p, pl.ds(BASE - WEIGHT_EDGE, WEIGHT_EDGE), :] = jnp.zeros((WEIGHT_EDGE, LANES), jnp.float32)
        h[p, pl.ds(BASE + width, WEIGHT_EDGE), :] = jnp.zeros((WEIGHT_EDGE, LANES), jnp.float32)
    build_splines(splines)
    alive = [jnp.where(here > 0, 1.0, 0.0), jnp.where(here < count - 1, 1.0, 0.0)]

    pl.semaphore_wait(barrier, count - 1)
    share(lambda p: pack, pool.at[me], psf_send.at[0], psf_recv.at[0])

    def move(n, first=1, last=count):
        source = moving[n]
        share(lambda p: source.at[:, columns(place(p))], landed.at[n, stripe(me)],
              move_send.at[n], move_recv.at[n], first, last)

    move(0)
    move(2, 1, count // 2)

    others = pl.ds(0, count - 1)
    others_rows = pl.ds(0, (count - 1) * band)

    def arrived(n, ref):
        all_of(landed.at[n, others_rows], move_send.at[n], move_recv.at[n]).wait_recv()
        kept[n].wait()
        put(ref, BASE, landed[n].T)

    all_of(pool.at[others], psf_send.at[0], psf_recv.at[0]).wait()
    gather_taps(pool, turned, band, taps, taps_t)
    build_forward(taps_t, forward)
    arrived(0, g)
    start, g_arrive = edges(0, g, EDGE)
    start()
    move(2, count // 2, count)
    move(1)
    build_adjoint(taps, adjoint)
    g_arrive()
    outer = (80, 72, 64, 48)
    inner = (32, 24, 16, 0)
    blurred[...] = tile_blur(g, 0, width, forward, 1, moved)
    arrived(2, h)
    x_start, x_arrive = edges(1, x, EDGE)
    weight_start, weight_arrive = edges(2, h, WEIGHT_EDGE)

    def share_sums(sweep, moved):
        d, b, w = wide(moved, BASE, width), blurred[...], wide(h, BASE, width)

        def lanes(values):
            column = jnp.sum(values, axis=0, keepdims=True)
            return column[:, :LANES] + column[:, LANES:]

        sums[sweep, me] = jnp.concatenate([lanes(d * d), lanes(w * b * b)], axis=0)
        share(lambda p: sums.at[sweep, me], sums.at[sweep, me], sum_send.at[sweep], sum_recv.at[sweep])

    def step_of(sweep):
        all_of(sums.at[sweep, others], sum_send.at[sweep], sum_recv.at[sweep]).wait()
        totals = jnp.sum(jnp.sum(sums[sweep], axis=0), axis=1, keepdims=True)
        return totals[0:1] / totals[1:2]

    def chunks(reach):
        return [pl.ds(BASE - reach + n, 32) for n in range(0, width + 2 * reach, 32)]

    share_sums(0, g)
    cascade(g, d_levels, splines, width, outer, alive)
    arrived(1, x)
    x_start()
    weight_start()
    x_arrive()
    cascade(x, x_levels, splines, width, outer, alive)
    step = step_of(0)
    limits = [step * thresholds[k] for k in range(levels)]
    planes = [x] + [x_levels.at[k] for k in range(levels)]
    moves = [g] + [d_levels.at[k] for k in range(levels)]
    for rows in chunks(outer[-1]):
        for p in range(PARTS):
            value = thresholded(planes, moves, step, limits, p, rows)
            new[p, rows, :] = value
            change[p, rows, :] = value - x[p, rows, :]
    weight_arrive()
    n = width + 2 * WEIGHT_EDGE
    value = tile_blur(change, -WEIGHT_EDGE, n, forward, 1, moved)
    put(pushed, BASE - WEIGHT_EDGE, value * wide(h, BASE - WEIGHT_EDGE, n))
    reach = inner[0]
    n = width + 2 * reach
    value = tile_blur(pushed, -reach, n, adjoint, -1, moved) + wide(g, BASE - reach, n)
    value = jnp.concatenate(
        [value[:reach] * alive[0], value[reach : reach + width], value[reach + width :] * alive[1]], axis=0
    )
    put(descent, BASE - reach, value)
    blurred[...] = tile_blur(descent, 0, width, forward, 1, moved)
    share_sums(1, descent)
    cascade(new, x_levels, splines, width, inner, alive)
    cascade(descent, d_levels, splines, width, inner, alive)
    step = step_of(1)
    limits = [step * thresholds[k] for k in range(levels)]
    planes[0], moves[0] = new, descent
    for rows in chunks(0):
        for p in range(PARTS):
            change[p, rows, :] = thresholded(planes, moves, step, limits, p, rows)
    result[...] = wide(change, BASE, width).T
    share(lambda p: result.at[stripe(p)], out.at[:, columns(here)], out_send.at[0], out_recv.at[0])
    out[:, columns(here)] = result[stripe(me), :]
    for n in range(len(moving)):
        all_of(landed.at[n, others_rows], move_send.at[n], move_recv.at[n]).wait_send()
    all_of(result.at[others_rows], out_send.at[0], out_recv.at[0]).wait_send()
    all_of(out.at[:, pl.ds(0, (count - 1) * width)], out_send.at[0], out_recv.at[0]).wait_recv()


def tile_body(image_now, gradient, hessian_weight, psf_tiles, facet_of_row, tile_slot, thresholds):
    band, columns = image_now.shape
    levels = thresholds.shape[0]
    rows, scales = lax.axis_size("rows"), lax.axis_size("scales")
    count = rows * scales
    width = columns // count
    f32 = lambda *shape: pltpu.VMEM(shape, jnp.float32)
    b16 = lambda *shape: pltpu.VMEM(shape, jnp.bfloat16)
    sem = lambda *shape: pltpu.SemaphoreType.DMA(shape)
    smem = pl.BlockSpec(memory_space=pltpu.SMEM)
    plane = (PARTS, width + 2 * BASE, LANES)
    table = b16(2, TILE * HEIGHT, HEIGHT)
    moved = f32(TILE, PARTS, width + 2 * EDGE, LANES)
    return pl.pallas_call(
        functools.partial(tile_kernel, rows, scales),
        out_shape=jax.ShapeDtypeStruct((band, columns), jnp.float32),
        in_specs=[pl.BlockSpec(memory_space=pltpu.HBM)] * 3 + [VMEM] + [smem] * 3,
        out_specs=VMEM,
        scratch_shapes=[
            f32(3, HEIGHT, width), *[f32(*plane)] * 7, f32(levels, *plane), f32(levels, *plane),
            b16(levels, HEIGHT, HEIGHT),
            f32(3, LANES), f32(count, 3, LANES), f32(TILE * count, TILE * TILE),
            f32(2, HEIGHT, TILE * TILE), f32(2, TILE * TILE, HEIGHT), table, table, moved,
            f32(width, HEIGHT), f32(SUBITERS, count, 2, LANES), f32(HEIGHT, width),
            sem(1), sem(1), sem(3), sem(3), sem(3, 2), sem(3, 2), sem(SUBITERS), sem(SUBITERS), sem(1), sem(1), sem(3),
        ],
        compiler_params=pltpu.CompilerParams(
            collective_id=0, has_side_effects=True, vmem_limit_bytes=56 * 1024 * 1024
        ),
    )(image_now, gradient, hessian_weight, psf_tiles, facet_of_row, tile_slot, thresholds)


def body(image_now, *rest):
    band, columns = image_now.shape
    count = lax.axis_size("rows") * lax.axis_size("scales")
    levels = rest[-1].shape[0]
    whole = columns % (count * LANES) == 0 and columns // count >= LANES and band * count == HEIGHT and levels == 4
    return (tile_body if whole else stripe_body)(image_now, *rest)


def solution(mesh):
    band = P(AXES, None)
    in_specs = (band, band, band, band, P(AXES), P(), P())
    return jax.shard_map(body, mesh=mesh, in_specs=in_specs, out_specs=band, check_vma=False)
```
